128 devices in a mesh: dp: 16 (over y, x), seq: 8 (over z, core).
Axes of the slice: x: 4, y: 4, z: 4, core: 2. Of those that a mesh axis runs over, the one named last changes fastest.
Arguments:
- tokens_in: bfloat16 [16, 4096, 1024], P('dp', 'seq'), may hold values from -6 to 6
- user_ids: int32 [16, 4096], P('dp'), may hold values from 0 to 3, never falling along the last dimension, each value on 1 to 2048 neighbouring positions
- w_in: bfloat16 [1024, 2048], replicated, may hold values from -0.1875 to 0.1875
- w_out: bfloat16 [512, 1024], replicated, may hold values from -0.25 to 0.25
- cotangent: bfloat16 [16, 4096, 1024], P('dp', 'seq'), may hold values from -6 to 6
Outputs:
- output: bfloat16 [16, 4096, 1024], P('dp', 'seq')
- grad_tokens: bfloat16 [16, 4096, 1024], P('dp', 'seq')
- grad_w_in: float32 [1024, 2048], P(('dp', 'seq'))
- grad_w_out: float32 [512, 1024], P(None, ('dp', 'seq'))
The draws below stay inside these ranges and needn't reach their ends.
Inputs may be any that keep to these rules, and one draw needn't show every extreme that they name: `user_ids`: in each stream the user number never falls; each user holds 1 to 2048 consecutive events and some user holds exactly 2048.
All inputs are finite; a program needn't handle non-finite values.
Results may differ from the reference program's by a relative error of at most 0.015.
Values may be sent and summed in bfloat16 or wider, within the bound.
A program may use at most 128 MiB of HBM per device.

```python
import math
import jax
import jax.numpy as jnp
import numpy as np
from jax import lax

D = 1024
HEADS = 4
HD = 128
ROWS = 512
USERS = 4
HQ = 512
STREAM = 4096
MOST = 2048
N_DP = 16


def raised(entries, rng, source, target, blocks, factor):
    def block_of(axis_at):
        return (jnp.arange(entries.shape[axis_at]) // (entries.shape[axis_at] // blocks)).reshape((-1,) + (1,) * (entries.ndim - 1 - axis_at))

    first = jax.random.permutation(rng, blocks)[block_of(target)]
    other_side = (block_of(target) + blocks // 2) % blocks
    return jnp.where((block_of(source) == first) | (block_of(source) == other_side), factor * entries, entries)


def steps_of(rng, shape, shards, low, high):
    loudness = 1.0
    for position, blocks in shards:
        draws = jax.random.uniform(jax.random.fold_in(jax.random.fold_in(rng, 6), position), (blocks,), jnp.float32, low / len(shards), high / len(shards))
        loudness = loudness * jnp.repeat(jnp.exp(draws), shape[position] // blocks).reshape((-1,) + (1,) * (len(shape) - 1 - position))
    return loudness


def length_profile(count, total, bound, lean):
    loads = [(1 << 20) // math.isqrt(rank ** lean) + 1 for rank in range(2, count + 1)]
    spare, holding = total - bound - (count - 1), [1] * (count - 1)
    while spare > 0:
        candidates = [i for i in range(count - 1) if holding[i] < bound]
        pool, left = sum([loads[i] for i in candidates]), spare
        for i in candidates:
            extra = min(bound - holding[i], max(1, left * loads[i] // pool), spare)
            holding[i] = holding[i] + extra
            spare = spare - extra
    return np.array([bound] + holding)


def uneven_parts(own_key, amount, total, bound, lean):
    if amount == 2:
        one = jax.random.randint(own_key, (), max(1, total - bound), min(bound, total - 1) + 1)
        return jnp.stack([one, total - one])
    lengths = jnp.asarray(length_profile(amount, total, bound, lean), jnp.int32)
    couples = (amount - 1) // 2
    donor, receiver = lengths[1:1 + 2 * couples:2], lengths[2:2 + 2 * couples:2]
    margin = jnp.minimum(donor - 1, bound - receiver)
    shifted = jax.random.randint(jax.random.fold_in(own_key, 1), (couples,), 0, 1 << 20) % (margin + 1)
    lengths = lengths.at[1:1 + 2 * couples:2].set(donor - shifted).at[2:2 + 2 * couples:2].set(receiver + shifted)
    return lengths[jax.random.permutation(jax.random.fold_in(own_key, 2), amount)]


def gaussian(stream_key, dims, deviation, limit, cuts=(), held_as=jnp.bfloat16):
    result = deviation * jax.random.normal(stream_key, dims, jnp.float32)
    if cuts:
        result = result * steps_of(stream_key, dims, cuts, -0.22, 0.18)
    return jnp.clip(result, -limit, limit).astype(held_as)


def noise_with(stream_key, dims, scale, bound, shards, heavy, kind=jnp.bfloat16):
    array = scale * jax.random.normal(stream_key, dims, jnp.float32)
    if shards:
        array = array * steps_of(stream_key, dims, shards, -0.22, 0.18)
    return jnp.clip(raised(array, jax.random.fold_in(stream_key, 3), *heavy), -bound, bound).astype(kind)


def setup_inputs(seed: int = 0) -> dict:
    keys = jax.random.split(jax.random.key(seed), 6)
    tokens_in = noise_with(keys[0], (N_DP, STREAM, D), 1.0, 6.0, ((0, 16), (1, 8)), (1, 2, 8, 2.0))
    user_ids = jax.vmap(lambda own: jnp.searchsorted(jnp.cumsum(uneven_parts(own, USERS, STREAM, MOST, 2)), jnp.arange(STREAM), side="right"))(jax.random.split(keys[1], N_DP)).reshape((N_DP, STREAM)).astype(jnp.int32)
    w_in = gaussian(keys[2], (D, 4 * HQ), D ** -0.5, 0.1875)
    w_out = gaussian(keys[3], (HQ, D), HQ ** -0.5, 0.25)
    cotangent = noise_with(keys[4], (N_DP, STREAM, D), 1.0, 6.0, ((0, 16), (1, 8)), (1, 2, 8, 2.0))
    return dict(tokens_in=tokens_in, user_ids=user_ids, w_in=w_in, w_out=w_out, cotangent=cotangent)


epsilon = 1e-05

def normalize(values):
    center = values - lax.optimization_barrier(jnp.mean(values, axis=-1, keepdims=True))
    inverse = lax.rsqrt(lax.optimization_barrier(jnp.mean(center * center, axis=-1, keepdims=True)) + epsilon)
    return center * inverse

def norm_back(values, upstream):
    center = values - lax.optimization_barrier(jnp.mean(values, axis=-1, keepdims=True))
    inverse = lax.rsqrt(lax.optimization_barrier(jnp.mean(center * center, axis=-1, keepdims=True)) + epsilon)
    scaled = center * inverse
    return inverse * (upstream - lax.optimization_barrier(jnp.mean(upstream, axis=-1, keepdims=True)) - scaled * lax.optimization_barrier(jnp.mean(upstream * scaled, axis=-1, keepdims=True)))

def silu_slope(values):
    sigma = jax.nn.sigmoid(values)
    return sigma * (1.0 + values * (1.0 - sigma))

def reference(tokens_in, user_ids, w_in, w_out, cotangent):
    scale = 1.0 / math.sqrt(HD)
    window = MOST + ROWS
    blocks = STREAM // ROWS

    def one_stream(carry, inputs):
        tokens, id_table, upstream = inputs
        tokens_f = tokens.astype(jnp.float32)
        normed = normalize(tokens_f).astype(jnp.bfloat16)
        hidden = jnp.dot(normed, w_in, preferred_element_type=jnp.float32)
        active = jax.nn.silu(hidden).astype(jnp.bfloat16)
        gate_u = active[:, :HQ]
        value_heads = active[:, HQ:2 * HQ].astype(jnp.float32).reshape(STREAM, HEADS, HD)
        query_heads = active[:, 2 * HQ:3 * HQ].astype(jnp.float32).reshape(STREAM, HEADS, HD)
        key_heads = active[:, 3 * HQ:].astype(jnp.float32).reshape(STREAM, HEADS, HD)

        def block_parts(index):
            q_start = (index * ROWS).astype(jnp.int32)
            k_start = jnp.clip(q_start - MOST, 0, STREAM - window).astype(jnp.int32)
            query_block = lax.dynamic_slice_in_dim(query_heads, q_start, ROWS, 0)
            key_block = lax.dynamic_slice_in_dim(key_heads, k_start, window, 0)
            value_block = lax.dynamic_slice_in_dim(value_heads, k_start, window, 0)
            q_users = lax.dynamic_slice_in_dim(id_table, q_start, ROWS, 0)
            k_users = lax.dynamic_slice_in_dim(id_table, k_start, window, 0)
            q_pos = q_start + jnp.arange(ROWS, dtype=jnp.int32)
            k_pos = k_start + jnp.arange(window, dtype=jnp.int32)
            allowed = (q_users[:, None] == k_users[None, :]) & (k_pos[None, :] <= q_pos[:, None])
            mask = allowed.astype(jnp.float32)[None]
            scores = jnp.einsum('qhd,khd->hqk', query_block, key_block) * scale
            weights = (jax.nn.silu(scores) * mask).astype(jnp.bfloat16)
            return (q_start, k_start, query_block, key_block, value_block, mask, scores, weights)

        def forward_block(index):
            parts = block_parts(index)
            return jnp.einsum('hqk,khd->qhd', parts[7].astype(jnp.float32), parts[4])
        attended = lax.map(forward_block, jnp.arange(blocks, dtype=jnp.int32)).reshape(STREAM, HQ)
        normed_out = normalize(attended)
        gated = (normed_out * gate_u.astype(jnp.float32)).astype(jnp.bfloat16)
        output = (jnp.dot(gated, w_out, preferred_element_type=jnp.float32) + tokens_f).astype(jnp.bfloat16)
        grad_w_out = jnp.dot(gated.T, upstream, preferred_element_type=jnp.float32)
        grad_gated = jnp.dot(upstream, w_out.T, preferred_element_type=jnp.float32)
        grad_u = grad_gated * normed_out
        grad_normed = grad_gated * gate_u.astype(jnp.float32)
        grad_attended = norm_back(attended, grad_normed).astype(jnp.bfloat16)
        grad_heads = grad_attended.astype(jnp.float32).reshape(STREAM, HEADS, HD)

        def backward_block(state, index):
            grad_k, grad_v = state
            q_start, k_start, query_block, key_block, value_block, mask, scores, weights = block_parts(index)
            grad_block = lax.dynamic_slice_in_dim(grad_heads, q_start, ROWS, 0)
            part_v = jnp.einsum('hqk,qhd->khd', weights.astype(jnp.float32), grad_block)
            grad_weights = jnp.einsum('qhd,khd->hqk', grad_block, value_block)
            grad_scores = (grad_weights * silu_slope(scores) * mask).astype(jnp.bfloat16).astype(jnp.float32)
            part_q = jnp.einsum('hqk,khd->qhd', grad_scores, key_block) * scale
            part_k = jnp.einsum('hqk,qhd->khd', grad_scores, query_block) * scale
            grad_k = lax.dynamic_update_slice_in_dim(grad_k, lax.dynamic_slice_in_dim(grad_k, k_start, window, 0) + part_k, k_start, 0)
            grad_v = lax.dynamic_update_slice_in_dim(grad_v, lax.dynamic_slice_in_dim(grad_v, k_start, window, 0) + part_v, k_start, 0)
            return ((grad_k, grad_v), part_q)
        zero_heads = jnp.zeros((STREAM, HEADS, HD), jnp.float32)
        (grad_k, grad_v), grad_q = lax.scan(backward_block, (zero_heads, zero_heads), jnp.arange(blocks, dtype=jnp.int32))
        grad_q = grad_q.reshape(STREAM, HQ)
        grad_all = jnp.concatenate([grad_u, grad_v.reshape(STREAM, HQ), grad_q, grad_k.reshape(STREAM, HQ)], axis=1)
        grad_hidden = (grad_all * silu_slope(hidden)).astype(jnp.bfloat16)
        grad_w_in = jnp.dot(normed.T, grad_hidden, preferred_element_type=jnp.float32)
        grad_normed_in = jnp.dot(grad_hidden, w_in.T, preferred_element_type=jnp.float32)
        grad_tokens = (norm_back(tokens_f, grad_normed_in) + upstream.astype(jnp.float32)).astype(jnp.bfloat16)
        total_in, total_out = carry
        return ((total_in + grad_w_in, total_out + grad_w_out), (output, grad_tokens))
    start = (jnp.zeros((D, 4 * HQ), jnp.float32), jnp.zeros((HQ, D), jnp.float32))
    (total_in, total_out), (output, grad_tokens) = lax.scan(one_stream, start, (tokens_in, user_ids, cotangent))
    return (output, grad_tokens, total_in, total_out)
```

```python
import functools
import math

import jax
import jax.numpy as jnp
from jax import lax
from jax.experimental import pallas as pl
from jax.experimental.pallas import tpu as pltpu
from jax.sharding import PartitionSpec as P

HEADS = 4
HD = 128
F32 = jnp.float32
BF16 = jnp.bfloat16
NB = 5


def place():
    dp, seq = lax.axis_index("dp"), lax.axis_index("seq")
    return dp // 4, dp % 4, seq // 2, seq % 2


def device(y, x, z, core):
    return {"dp": y * 4 + x, "seq": z * 2 + core}


def turn(i, d):
    return lax.rem(i + d, 4)


def remote(src, dst, send, recv, target):
    return pltpu.make_async_remote_copy(
        src_ref=src, dst_ref=dst, send_sem=send, recv_sem=recv,
        device_id=target, device_id_type=pl.DeviceIdType.MESH)


def greet(targets):
    barrier = pltpu.get_barrier_semaphore()
    for t in targets:
        pl.semaphore_signal(barrier, inc=1, device_id=t, device_id_type=pl.DeviceIdType.MESH)
    pl.semaphore_wait(barrier, len(targets))


def reduce_kernel(normed, gh, gated, cot, out_in, out_out,
                  part, send1, recv1, s2, r2a, r2b, s3a, s3b, r3a, r3b, t4, r4,
                  ss1, rs1, ss2, rs2, ss3, rs3, ss4, rs4):
    y, x, z, c = place()
    other = 1 - c
    greet([device(y, x, z, other)]
          + [device(y, turn(x, d), z, c) for d in (1, 2, 3)]
          + [device(turn(y, d), x, z, c) for d in (1, 2, 3)]
          + [device(y, x, turn(z, d), c) for d in (1, 2, 3)])

    def contract(a, b):
        return lax.dot_general(a, b, (((0,), (0,)), ((), ())), preferred_element_type=F32)

    copies1 = []
    for b in range(NB):
        for r in range(4):
            rows = pl.ds(r * 256, 256)
            if b == 0:
                p = contract(cot[:, rows], gated[...])
            else:
                p = contract(normed[:, rows], gh[:, (b - 1) * 512:b * 512])
            part[b, r * 16:(r + 1) * 16] = p.reshape(16, 2, 8, 512)
        send1[b] = part[b, :, other].reshape(512, 512).astype(BF16)
        cp = remote(send1.at[b], recv1.at[b], ss1.at[b], rs1.at[b], device(y, x, z, other))
        cp.start()
        copies1.append(cp)

    copies2 = []
    for b in range(NB):
        copies1[b].wait()
        s = part[b, :, c].reshape(512, 512) + recv1[b].astype(F32)
        s2[b] = s.astype(BF16).reshape(4, 4, 32, 512)
        for d in (1, 2, 3):
            xx, yy = turn(x, d), turn(y, d)
            ca = remote(s2.at[b, :, xx, :, pl.ds(0, 256)], r2a.at[b, d - 1], ss2.at[b, d - 1],
                        rs2.at[b, d - 1], device(y, xx, z, c))
            cb = remote(s2.at[b, yy, :, :, pl.ds(256, 256)], r2b.at[b, d - 1], ss2.at[b, d + 2],
                        rs2.at[b, d + 2], device(yy, x, z, c))
            ca.start()
            cb.start()
            copies2.append(ca)
            copies2.append(cb)

    copies3 = []
    for b in range(NB):
        for cp in copies2[6 * b:6 * b + 6]:
            cp.wait()
        a = s2[b, :, x, :, 0:256].astype(F32)
        e = s2[b, y, :, :, 256:512].astype(F32)
        for d in range(3):
            a = a + r2a[b, d].astype(F32)
            e = e + r2b[b, d].astype(F32)
        s3a[b] = a.astype(BF16)
        s3b[b] = e.astype(BF16)
        for d in (1, 2, 3):
            xx, yy = turn(x, d), turn(y, d)
            ca = remote(s3a.at[b, yy], r3a.at[b, d - 1], ss3.at[b, d - 1], rs3.at[b, d - 1],
                        device(yy, x, z, c))
            cb = remote(s3b.at[b, xx], r3b.at[b, d - 1], ss3.at[b, d + 2], rs3.at[b, d + 2],
                        device(y, xx, z, c))
            ca.start()
            cb.start()
            copies3.append(ca)
            copies3.append(cb)

    for b in range(NB):
        for cp in copies3[6 * b:6 * b + 6]:
            cp.wait()
        a = s3a[b, y].astype(F32)
        e = s3b[b, x].astype(F32)
        for d in range(3):
            a = a + r3a[b, d].astype(F32)
            e = e + r3b[b, d].astype(F32)
        t4[:, :, b * 512:b * 512 + 256] = a.reshape(4, 8, 256)
        t4[:, :, b * 512 + 256:b * 512 + 512] = e.reshape(4, 8, 256)
    copies4 = []
    for d in (1, 2, 3):
        zz = turn(z, d)
        cp = remote(t4.at[zz], r4.at[d - 1], ss4.at[d - 1], rs4.at[d - 1], device(y, x, zz, c))
        cp.start()
        copies4.append(cp)
    for cp in copies4:
        cp.wait()
    total = t4[z] + r4[0] + r4[1] + r4[2]
    out_out[...] = total[:, 0:512]
    out_in[...] = total[:, 512:2560]


def reduce_weights(normed, grad_hidden, gated, upstream):
    vmem = pl.BlockSpec(memory_space=pltpu.VMEM)
    dma = pltpu.SemaphoreType.DMA
    total_in, total_out = pl.pallas_call(
        reduce_kernel,
        name="reduce_weights",
        out_shape=(jax.ShapeDtypeStruct((8, 2048), F32), jax.ShapeDtypeStruct((8, 512), F32)),
        in_specs=[vmem] * 4,
        out_specs=(vmem, vmem),
        scratch_shapes=[
            pltpu.VMEM((NB, 64, 2, 8, 512), F32),
            pltpu.VMEM((NB, 512, 512), BF16),
            pltpu.VMEM((NB, 512, 512), BF16),
            pltpu.VMEM((NB, 4, 4, 32, 512), BF16),
            pltpu.VMEM((NB, 3, 4, 32, 256), BF16),
            pltpu.VMEM((NB, 3, 4, 32, 256), BF16),
            pltpu.VMEM((NB, 4, 32, 256), BF16),
            pltpu.VMEM((NB, 4, 32, 256), BF16),
            pltpu.VMEM((NB, 3, 32, 256), BF16),
            pltpu.VMEM((NB, 3, 32, 256), BF16),
            pltpu.VMEM((4, 8, NB * 512), F32),
            pltpu.VMEM((3, 8, NB * 512), F32),
            dma((NB,)), dma((NB,)), dma((NB, 6)), dma((NB, 6)), dma((NB, 6)), dma((NB, 6)),
            dma((3,)), dma((3,)),
        ],
        compiler_params=pltpu.CompilerParams(
            collective_id=0, has_side_effects=True, vmem_limit_bytes=56 * 1024 * 1024),
    )(normed, grad_hidden, gated, upstream)
    return total_in, total_out.T


epsilon = 1e-05


def from_behind(value, axis, by):
    devices = lax.axis_size(axis)
    pairs = [(i, i + by) for i in range(devices) if 0 <= i + by < devices]
    return lax.ppermute(value, axis, pairs)


def normalize(values):
    center = values - jnp.mean(values, axis=-1, keepdims=True)
    inverse = lax.rsqrt(jnp.mean(center * center, axis=-1, keepdims=True) + epsilon)
    return center * inverse


def norm_back(values, upstream):
    center = values - jnp.mean(values, axis=-1, keepdims=True)
    inverse = lax.rsqrt(jnp.mean(center * center, axis=-1, keepdims=True) + epsilon)
    scaled = center * inverse
    return inverse * (
        upstream
        - jnp.mean(upstream, axis=-1, keepdims=True)
        - scaled * jnp.mean(upstream * scaled, axis=-1, keepdims=True)
    )


def silu_slope(values):
    sigma = jax.nn.sigmoid(values)
    return sigma * (1.0 + values * (1.0 - sigma))


def local(tokens_in, user_ids, w_in, w_out, cotangent):
    tokens = tokens_in[0]
    id_table = user_ids[0]
    upstream = cotangent[0]
    n_rows = tokens.shape[0]
    width = w_out.shape[0]
    span = lax.axis_size("seq") // 2
    q_start = lax.axis_index("seq") * n_rows
    scale = 1.0 / math.sqrt(HD)
    tokens_f = tokens.astype(jnp.float32)
    normed = normalize(tokens_f).astype(jnp.bfloat16)
    hidden = jnp.dot(normed, w_in, preferred_element_type=jnp.float32)
    active = jax.nn.silu(hidden).astype(jnp.bfloat16)
    gate_u = active[:, :width]
    values_own = active[:, width : 2 * width]
    query = active[:, 2 * width : 3 * width]
    keys_own = active[:, 3 * width :]
    query_heads = query.reshape(n_rows, HEADS, HD)
    my_users = lax.dynamic_slice_in_dim(id_table, q_start, n_rows)
    q_pos = q_start + jnp.arange(n_rows, dtype=jnp.int32)

    def key_mask(start):
        k_pos = start + jnp.arange(n_rows, dtype=jnp.int32)
        k_users = lax.dynamic_slice_in_dim(id_table, jnp.maximum(start, 0), n_rows)
        allowed = (
            (k_pos[None, :] >= 0)
            & (k_users[None, :] == my_users[:, None])
            & (k_pos[None, :] <= q_pos[:, None])
        )
        return allowed.astype(jnp.float32)[None]

    pieces = []
    pieces.append((keys_own, values_own, q_start))
    for distance in range(1, span + 1):
        keys_far, values_far = from_behind((keys_own, values_own), "seq", distance)
        pieces.append((keys_far, values_far, q_start - distance * n_rows))
    attended = jnp.zeros((n_rows, HEADS, HD), jnp.float32)
    for piece_keys, piece_values, start in pieces:
        key_heads = piece_keys.reshape(n_rows, HEADS, HD)
        value_heads = piece_values.reshape(n_rows, HEADS, HD)
        scores = (
            jnp.einsum("qhd,khd->hqk", query_heads, key_heads, preferred_element_type=jnp.float32)
            * scale
        )
        weights = (jax.nn.silu(scores) * key_mask(start)).astype(jnp.bfloat16)
        attended = attended + jnp.einsum(
            "hqk,khd->qhd", weights, value_heads, preferred_element_type=jnp.float32
        )
    attended = attended.reshape(n_rows, width)
    normed_out = normalize(attended)
    gated = (normed_out * gate_u.astype(jnp.float32)).astype(jnp.bfloat16)
    output = (jnp.dot(gated, w_out, preferred_element_type=jnp.float32) + tokens_f).astype(
        jnp.bfloat16
    )
    grad_gated = jnp.dot(upstream, w_out.T, preferred_element_type=jnp.float32)
    grad_u = grad_gated * normed_out
    grad_normed = grad_gated * gate_u.astype(jnp.float32)
    grad_attended = norm_back(attended, grad_normed).astype(jnp.bfloat16)
    grad_heads = grad_attended.reshape(n_rows, HEADS, HD)
    grad_query = jnp.zeros((n_rows, HEADS, HD), jnp.float32)
    key_terms = []
    for piece_keys, piece_values, start in pieces:
        key_heads = piece_keys.reshape(n_rows, HEADS, HD)
        value_heads = piece_values.reshape(n_rows, HEADS, HD)
        mask = key_mask(start)
        scores = (
            jnp.einsum("qhd,khd->hqk", query_heads, key_heads, preferred_element_type=jnp.float32)
            * scale
        )
        weights = (jax.nn.silu(scores) * mask).astype(jnp.bfloat16)
        part_values = jnp.einsum(
            "hqk,qhd->khd", weights, grad_heads, preferred_element_type=jnp.float32
        )
        grad_weights = jnp.einsum(
            "qhd,khd->hqk", grad_heads, value_heads, preferred_element_type=jnp.float32
        )
        grad_scores = (grad_weights * silu_slope(scores) * mask).astype(jnp.bfloat16)
        grad_query = (
            grad_query
            + jnp.einsum("hqk,khd->qhd", grad_scores, key_heads, preferred_element_type=jnp.float32)
            * scale
        )
        part_keys = (
            jnp.einsum("hqk,qhd->khd", grad_scores, query_heads, preferred_element_type=jnp.float32)
            * scale
        )
        key_terms.append(
            (part_keys.reshape(n_rows, width), part_values.reshape(n_rows, width), start)
        )
    grad_keys = key_terms[0][0]
    grad_values = key_terms[0][1]
    for distance in range(1, span + 1):
        back_keys, back_values = (
            from_behind(key_terms[distance][0].astype(jnp.bfloat16), "seq", -distance).astype(
                jnp.float32
            ),
            from_behind(key_terms[distance][1].astype(jnp.bfloat16), "seq", -distance).astype(
                jnp.float32
            ),
        )
        grad_keys = grad_keys + back_keys
        grad_values = grad_values + back_values
    grad_all = jnp.concatenate(
        [grad_u, grad_values, grad_query.reshape(n_rows, width), grad_keys], axis=1
    )
    grad_hidden = (grad_all * silu_slope(hidden)).astype(jnp.bfloat16)
    grad_normed_in = jnp.dot(grad_hidden, w_in.T, preferred_element_type=jnp.float32)
    grad_tokens = (norm_back(tokens_f, grad_normed_in) + upstream.astype(jnp.float32)).astype(
        jnp.bfloat16
    )
    total_in, total_out = reduce_weights(normed, grad_hidden, gated, upstream)
    return (output[None], grad_tokens[None], total_in, total_out)


def solution(mesh):
    in_specs = (P("dp", "seq", None), P("dp", None), P(), P(), P("dp", "seq", None))
    out_specs = (
        P("dp", "seq", None),
        P("dp", "seq", None),
        P(("dp", "seq"), None),
        P(None, ("dp", "seq")),
    )
    return jax.shard_map(local, mesh=mesh, in_specs=in_specs, out_specs=out_specs, check_vma=False)
```

```python
import math

import jax
import jax.numpy as jnp
from jax import lax
from jax.experimental import pallas as pl
from jax.experimental.pallas import tpu as pltpu
from jax.sharding import PartitionSpec as P

HEADS = 4
HD = 128
ROWS = 512
F32 = jnp.float32
BF16 = jnp.bfloat16
EPS = 1e-05
HALF_SCALE = 0.5 / math.sqrt(HD)
MESH = pl.DeviceIdType.MESH
NB = 5

OWN_MOVES = (
    (0, 1, 0, (0, 1, 2, 3)),
    (0, 3, 0, (2, 3)),
    (1, 2, 1, (0, 1, 2)),
    (1, 0, 1, (3, 1, 2)),
    (2, 3, 2, (0, 1, 2, 3)),
)
RELAYS = {
    (1, 0, 0): 2, (1, 0, 1): 2,
    (0, 1, 3): 3, (0, 1, 1): 3, (0, 1, 2): 3,
    (3, 0, 2): 2, (3, 0, 3): 2, (3, 1, 3): 2,
    (2, 1, 0): 3,
}
ARRIVALS = {
    0: ((1, 3), (1, 1), (1, 2)),
    1: ((0, 0), (0, 1), (0, 2), (0, 3)),
    2: ((1, 0), (1, 1), (0, 2), (1, 2), (0, 3), (0, 0), (1, 3), (0, 1)),
    3: ((2, 0), (0, 2), (2, 1), (0, 3), (2, 2), (1, 3), (2, 3), (1, 1), (1, 2), (1, 0)),
}
STEPS = 10


def place():
    dp, seq = lax.axis_index("dp"), lax.axis_index("seq")
    return dp // 4, dp % 4, seq // 2, seq % 2


def device(y, x, z, core):
    return {"dp": y * 4 + x, "seq": z * 2 + core}


def turn(i, d):
    return lax.rem(i + d, 4)


def remote(src, dst, send, recv, target):
    return pltpu.make_async_remote_copy(
        src_ref=src, dst_ref=dst, send_sem=send, recv_sem=recv,
        device_id=target, device_id_type=MESH)


def dot_nn(a, b):
    return jnp.dot(a, b, preferred_element_type=F32)


def dot_nt(a, b):
    return lax.dot_general(a, b, (((1,), (1,)), ((), ())), preferred_element_type=F32)


def dot_tn(a, b):
    return lax.dot_general(a, b, (((0,), (0,)), ((), ())), preferred_element_type=F32)


class Gather:
    def __init__(self, near, far, sems, chip, core, target):
        self.near, self.far = near, far
        self.ss, self.rs, self.sp, self.rp = sems
        self.chip, self.core, self.target = chip, core, target

    def move(self, sender, receiver, owner, h):
        k = 0 if receiver == sender + 1 else 1
        return remote(self.near.at[owner, h], self.near.at[owner, h], self.ss.at[owner, h, k],
                      self.rs.at[owner, h], self.target(receiver, self.core))

    def share(self, owner, h):
        return remote(self.near.at[owner, h], self.far.at[owner, h], self.sp.at[owner, h],
                      self.rp.at[owner, h], self.target(self.chip, 1 - self.core))

    def start(self):
        @pl.when(self.core == 0)
        def _():
            for h in range(HEADS):
                self.share(self.chip, h).start()
        for sender, receiver, owner, heads in OWN_MOVES:
            @pl.when(self.chip == sender)
            def _():
                for h in heads:
                    self.move(sender, receiver, owner, h).start()

    def arrive(self, step):
        for role, order in ARRIVALS.items():
            if step >= len(order):
                continue
            owner, h = order[step]

            @pl.when(self.chip == role)
            def _():
                self.move(role, (role + 1) % 4, owner, h).wait_recv()
                if (role, owner, h) in RELAYS:
                    self.move(role, RELAYS[role, owner, h], owner, h).start()
                if owner == role - 1:
                    self.share(owner, h).start()
                if owner == role - 2:
                    @pl.when(self.core == 1)
                    def _():
                        self.share(owner, h).start()

    def drain(self):
        @pl.when(self.core == 0)
        def _():
            for h in range(HEADS):
                self.share(self.chip, h).wait_send()
        for sender, receiver, owner, heads in OWN_MOVES:
            @pl.when(self.chip == sender)
            def _():
                for h in heads:
                    self.move(sender, receiver, owner, h).wait_send()
        for (role, owner, h), receiver in RELAYS.items():
            @pl.when(self.chip == role)
            def _():
                self.move(role, receiver, owner, h).wait_send()
        for role, order in ARRIVALS.items():
            for owner, h in order:
                if owner == role - 1:
                    @pl.when(self.chip == role)
                    def _():
                        self.share(owner, h).wait_send()
                if owner == role - 2:
                    @pl.when((self.chip == role) & (self.core == 1))
                    def _():
                        self.share(owner, h).wait_send()

    def block(self, d):
        if d == 0:
            return self.near, self.chip
        if d % 2 == 0:
            return self.near, self.chip - d // 2
        return self.far, self.chip - (d + 1) // 2 + self.core

    def wait_share(self, d, h):
        if d % 2 == 1:
            owner = self.chip - (d + 1) // 2 + self.core
            self.share(owner, h).wait_recv()


def layer_kernel(tokens, ids, w_in, w_out, cot, output, grad_tokens, out_in, out_out,
                 normed, slope, u, kv, kv2, qs, qs2, gs, gs2, att, dq, dk, dv, gated, gh, masks, masks_t,
                 tmp, part, s2, recv1, r2a, r2b, s3a, s3b, r3a, r3b, t4, r4,
                 kss, krs, ksp, krp, qss, qrs, qsp, qrp, gss, grs, gsp, grp,
                 ss1, rs1, ss2, rs2, ss3, rs3, ss4, rs4):
    y, x, z, c = place()
    other = 1 - c
    block = z * 2 + c
    peers = ([device(y, x, z, other)]
             + [device(y, turn(x, d), z, c) for d in (1, 2, 3)]
             + [device(turn(y, d), x, z, c) for d in (1, 2, 3)]
             + [device(y, x, turn(z, d), c) for d in (1, 2, 3)])
    barrier = pltpu.get_barrier_semaphore()
    for t in peers:
        pl.semaphore_signal(barrier, inc=1, device_id=t, device_id_type=MESH)

    before = Gather(kv, kv2, (kss, krs, ksp, krp), z, c, lambda zz, cc: device(y, x, zz, cc))
    mz, mc = 3 - z, 1 - c

    def mirrored(zz, cc):
        return device(y, x, 3 - zz, 1 - cc)

    queries = Gather(qs, qs2, (qss, qrs, qsp, qrp), mz, mc, mirrored)
    grads = Gather(gs, gs2, (gss, grs, gsp, grp), mz, mc, mirrored)

    def stats(v):
        center = v - jnp.mean(v, axis=-1, keepdims=True)
        inverse = lax.rsqrt(jnp.mean(center * center, axis=-1, keepdims=True) + EPS)
        return center * inverse, inverse

    def row_loop(size):
        def wrap(body):
            @pl.loop(0, ROWS // size)
            def _(i):
                body(pl.ds(pl.multiple_of(i * size, size), size))
        return wrap

    @row_loop(128)
    def _(rows):
        normed[rows, :] = stats(tokens[rows, :].astype(F32))[0].astype(BF16)

    def features(col, put):
        @row_loop(256)
        def _(rows):
            half = 0.5 * dot_nn(normed[rows, :], w_in[:, col:col + 512])
            t = jnp.tanh(half)
            slope[rows, col:col + 512] = 0.5 * (1.0 + t) * (1.0 + half * (1.0 - t))
            put(rows, (half * (1.0 + t)).astype(BF16))

    def put_k(rows, a):
        for h in range(HEADS):
            kv[z, h, rows, 0:128] = a[:, h * 128:(h + 1) * 128]

    def put_v(rows, a):
        for h in range(HEADS):
            kv[z, h, rows, 128:256] = a[:, h * 128:(h + 1) * 128]

    def put_q(rows, a):
        for h in range(HEADS):
            qs[mz, h, rows, :] = a[:, h * 128:(h + 1) * 128]

    def put_u(rows, a):
        u[rows, :] = a

    features(1536, put_k)
    features(512, put_v)
    pl.semaphore_wait(barrier, len(peers))
    before.start()
    features(1024, put_q)
    features(0, put_u)

    def ids_of(b):
        b = jnp.clip(b, 0, 7)
        return ids[:, pl.ds(pl.multiple_of(b * ROWS, ROWS), ROWS)].astype(F32)

    own_ids = jnp.transpose(jnp.broadcast_to(ids_of(block), (128, ROWS)))
    own_col = jnp.broadcast_to(own_ids[:, 0:1], (ROWS, ROWS))
    one, nil = jnp.ones((ROWS, ROWS), F32), jnp.zeros((ROWS, ROWS), F32)
    down = lax.broadcasted_iota(jnp.int32, (ROWS, ROWS), 0)
    right = lax.broadcasted_iota(jnp.int32, (ROWS, ROWS), 1)
    for d in range(5):
        same = own_col == jnp.broadcast_to(ids_of(block - d), (ROWS, ROWS))
        same_t = own_col == jnp.broadcast_to(ids_of(block + d), (ROWS, ROWS))
        if d == 0:
            same = same & (right <= down)
            same_t = same_t & (down <= right)
        masks[d] = jnp.where(same, one, nil).astype(BF16)
        masks_t[d] = jnp.where(same_t, one, nil).astype(BF16)

    def spans(d, flip):
        if d == 0:
            pair = ((0, 256), (0, 512)) if not flip else ((0, 512), (256, 512))
        elif d == 4:
            pair = ((0, 512), (256, 512)) if not flip else ((0, 256), (0, 512))
        else:
            pair = ((0, 512), (0, 512))
        return ((0, 256) + pair[0], (256, 512) + pair[1])

    def forward(d):
        @pl.when(block >= d)
        def _():
            ref, i = before.block(d)

            @pl.loop(0, HEADS)
            def _(h):
                before.wait_share(d, h)
                for r0, r1, c0, c1 in spans(d, False):
                    half = dot_nt(qs[mz, h, r0:r1, :], ref[i, h, c0:c1, 0:128]) * HALF_SCALE
                    w = (half * (1.0 + jnp.tanh(half))).astype(BF16) * masks[d, r0:r1, c0:c1]
                    a = dot_nn(w, ref[i, h, c0:c1, 128:256])
                    if d == 0:
                        att[h, r0:r1, :] = a
                    else:
                        att[h, r0:r1, :] += a

    def query_back(d):
        @pl.when(block >= d)
        def _():
            ref, i = before.block(d)

            @pl.loop(0, HEADS)
            def _(h):
                for r0, r1, c0, c1 in spans(d, False):
                    half = dot_nt(qs[mz, h, r0:r1, :], ref[i, h, c0:c1, 0:128]) * HALF_SCALE
                    t = jnp.tanh(half)
                    dw = dot_nt(gs[mz, h, r0:r1, :], ref[i, h, c0:c1, 128:256])
                    ds = (dw * ((1.0 + t) * (1.0 + half * (1.0 - t)))).astype(BF16) * masks[d, r0:r1, c0:c1]
                    a = dot_nn(ds, ref[i, h, c0:c1, 0:128])
                    if d == 0:
                        dq[h, r0:r1, :] = a
                    else:
                        dq[h, r0:r1, :] += a

    def key_back(d):
        @pl.when(block + d <= 7)
        def _():
            qref, i = queries.block(d)
            gref, _ = grads.block(d)

            @pl.loop(0, HEADS)
            def _(h):
                queries.wait_share(d, h)
                grads.wait_share(d, h)
                for r0, r1, c0, c1 in spans(d, True):
                    qq, gg = qref[i, h, c0:c1, :], gref[i, h, c0:c1, :]
                    half = dot_nt(kv[z, h, r0:r1, 0:128], qq) * HALF_SCALE
                    t = jnp.tanh(half)
                    m = masks_t[d, r0:r1, c0:c1]
                    w = (half * (1.0 + t)).astype(BF16) * m
                    dw = dot_nt(kv[z, h, r0:r1, 128:256], gg)
                    ds = (dw * ((1.0 + t) * (1.0 + half * (1.0 - t)))).astype(BF16) * m
                    av, ak = dot_nn(w, gg), dot_nn(ds, qq)
                    if d == 0:
                        dv[h, r0:r1, :] = av
                        dk[h, r0:r1, :] = ak
                    else:
                        dv[h, r0:r1, :] += av
                        dk[h, r0:r1, :] += ak

    def pair_copy(b):
        return remote(s2.at[b], recv1.at[b], ss1.at[b], rs1.at[b], device(y, x, z, other))

    def weight(b, left, cols):
        @pl.loop(0, 4)
        def _(r):
            rows = pl.ds(pl.multiple_of(r * 256, 256), 256)
            tmp[...] = dot_tn(left[:, rows], cols).reshape(16, 2, 8, 512)
            half = pl.ds(pl.multiple_of(r * 128, 128), 128)
            part[b, half, :] = tmp[:, c].reshape(128, 512)
            s2[b, r] = tmp[:, other].reshape(4, 32, 512).astype(BF16)
        pair_copy(b).start()

    def plane_copies(b):
        out = []
        for d in (1, 2, 3):
            xx, yy = turn(x, d), turn(y, d)
            out.append(remote(s2.at[b, :, xx, :, pl.ds(0, 256)], r2a.at[b, d - 1], ss2.at[b, d - 1],
                              rs2.at[b, d - 1], device(y, xx, z, c)))
            out.append(remote(s2.at[b, yy, :, :, pl.ds(256, 256)], r2b.at[b, d - 1], ss2.at[b, d + 2],
                              rs2.at[b, d + 2], device(yy, x, z, c)))
        return out

    def line_copies(b):
        out = []
        for d in (1, 2, 3):
            xx, yy = turn(x, d), turn(y, d)
            out.append(remote(s3a.at[b, yy], r3a.at[b, d - 1], ss3.at[b, d - 1], rs3.at[b, d - 1],
                              device(yy, x, z, c)))
            out.append(remote(s3b.at[b, xx], r3b.at[b, d - 1], ss3.at[b, d + 2], rs3.at[b, d + 2],
                              device(y, xx, z, c)))
        return out

    def second(b):
        pair_copy(b).wait()
        for i in range(4):
            mine = part[b, i * 128:(i + 1) * 128, :].reshape(4, 32, 512)
            s2[b, i] = (mine + recv1[b, i].astype(F32)).astype(BF16)
        for cp in plane_copies(b):
            cp.start()

    def third(b):
        for cp in plane_copies(b):
            cp.wait()
        a = s2[b, :, x, :, 0:256].astype(F32)
        e = s2[b, y, :, :, 256:512].astype(F32)
        for d in range(3):
            a = a + r2a[b, d].astype(F32)
            e = e + r2b[b, d].astype(F32)
        s3a[b] = a.astype(BF16)
        s3b[b] = e.astype(BF16)
        for cp in line_copies(b):
            cp.start()

    def fourth(b):
        for cp in line_copies(b):
            cp.wait()
        a = s3a[b, y].astype(F32)
        e = s3b[b, x].astype(F32)
        for d in range(3):
            a = a + r3a[b, d].astype(F32)
            e = e + r3b[b, d].astype(F32)
        t4[:, :, b * 512:b * 512 + 256] = a.reshape(4, 8, 256)
        t4[:, :, b * 512 + 256:b * 512 + 512] = e.reshape(4, 8, 256)

    forward(0)
    for step in range(STEPS):
        before.arrive(step)
    queries.start()
    for d in range(1, 5):
        forward(d)

    @row_loop(256)
    def _(rows):
        a = jnp.concatenate([att[h, rows, :] for h in range(HEADS)], axis=1)
        no, inverse = stats(a)
        uu = u[rows, :].astype(F32)
        g = (no * uu).astype(BF16)
        gated[rows, :] = g
        output[rows, :] = (dot_nn(g, w_out[...]) + tokens[rows, :].astype(F32)).astype(BF16)
        gg = dot_nt(cot[rows, :], w_out[...])
        gh[rows, 0:512] = (gg * no * slope[rows, 0:512]).astype(BF16)
        gn = gg * uu
        back = inverse * (gn - jnp.mean(gn, axis=-1, keepdims=True)
                          - no * jnp.mean(gn * no, axis=-1, keepdims=True))
        back = back.astype(BF16)
        for h in range(HEADS):
            gs[mz, h, rows, :] = back[:, h * 128:(h + 1) * 128]

    grads.start()
    weight(0, cot, gated[...])
    weight(1, normed, gh[:, 0:512])
    query_back(0)
    for step in range(STEPS):
        queries.arrive(step)
    second(0)
    second(1)
    for d in range(1, 5):
        query_back(d)

    @row_loop(256)
    def _(rows):
        for h in range(HEADS):
            at = 1024 + h * 128
            gh[rows, at:at + 128] = (dq[h, rows, :] * HALF_SCALE * slope[rows, at:at + 128]).astype(BF16)

    weight(3, normed, gh[:, 1024:1536])
    key_back(0)
    second(3)
    for step in range(STEPS):
        grads.arrive(step)
    third(0)
    third(1)
    for d in range(1, 5):
        key_back(d)

    @row_loop(256)
    def _(rows):
        for h in range(HEADS):
            at = 512 + h * 128
            gh[rows, at:at + 128] = (dv[h, rows, :] * slope[rows, at:at + 128]).astype(BF16)
            at = 1536 + h * 128
            gh[rows, at:at + 128] = (dk[h, rows, :] * HALF_SCALE * slope[rows, at:at + 128]).astype(BF16)

    weight(2, normed, gh[:, 512:1024])
    weight(4, normed, gh[:, 1536:2048])
    third(3)
    second(2)
    second(4)

    @row_loop(256)
    def _(rows):
        up = dot_nt(gh[rows, :], w_in[...])
        zhat, inverse = stats(tokens[rows, :].astype(F32))
        back = inverse * (up - jnp.mean(up, axis=-1, keepdims=True)
                          - zhat * jnp.mean(up * zhat, axis=-1, keepdims=True))
        grad_tokens[rows, :] = (back + cot[rows, :].astype(F32)).astype(BF16)

    fourth(0)
    fourth(1)
    fourth(3)
    third(2)
    third(4)
    fourth(2)
    fourth(4)
    last = []
    for d in (1, 2, 3):
        zz = turn(z, d)
        cp = remote(t4.at[zz], r4.at[d - 1], ss4.at[d - 1], rs4.at[d - 1], device(y, x, zz, c))
        cp.start()
        last.append(cp)
    before.drain()
    queries.drain()
    grads.drain()
    for cp in last:
        cp.wait()
    total = t4[z] + r4[0] + r4[1] + r4[2]
    out_out[...] = total[:, 0:512]
    out_in[...] = total[:, 512:2560]


def local(tokens_in, user_ids, w_in, w_out, cotangent):
    vmem = pl.BlockSpec(memory_space=pltpu.VMEM)
    dma = pltpu.SemaphoreType.DMA

    def gather_sems():
        return [dma((4, 4, 2)), dma((4, 4)), dma((4, 4)), dma((4, 4))]

    output, grad_tokens, total_in, total_out = pl.pallas_call(
        layer_kernel,
        name="layer",
        out_shape=(
            jax.ShapeDtypeStruct((ROWS, 1024), BF16),
            jax.ShapeDtypeStruct((ROWS, 1024), BF16),
            jax.ShapeDtypeStruct((8, 2048), F32),
            jax.ShapeDtypeStruct((8, 512), F32),
        ),
        in_specs=[vmem] * 5,
        out_specs=(vmem,) * 4,
        scratch_shapes=[
            pltpu.VMEM((ROWS, 1024), BF16),
            pltpu.VMEM((ROWS, 2048), F32),
            pltpu.VMEM((ROWS, 512), BF16),
            pltpu.VMEM((4, 4, ROWS, 256), BF16),
            pltpu.VMEM((4, 4, ROWS, 256), BF16),
            pltpu.VMEM((4, 4, ROWS, 128), BF16),
            pltpu.VMEM((4, 4, ROWS, 128), BF16),
            pltpu.VMEM((4, 4, ROWS, 128), BF16),
            pltpu.VMEM((4, 4, ROWS, 128), BF16),
            pltpu.VMEM((4, ROWS, 128), F32),
            pltpu.VMEM((4, ROWS, 128), F32),
            pltpu.VMEM((4, ROWS, 128), F32),
            pltpu.VMEM((4, ROWS, 128), F32),
            pltpu.VMEM((ROWS, 512), BF16),
            pltpu.VMEM((ROWS, 2048), BF16),
            pltpu.VMEM((5, ROWS, ROWS), BF16),
            pltpu.VMEM((5, ROWS, ROWS), BF16),
            pltpu.VMEM((16, 2, 8, 512), F32),
            pltpu.VMEM((NB, 512, 512), F32),
            pltpu.VMEM((NB, 4, 4, 32, 512), BF16),
            pltpu.VMEM((NB, 4, 4, 32, 512), BF16),
            pltpu.VMEM((NB, 3, 4, 32, 256), BF16),
            pltpu.VMEM((NB, 3, 4, 32, 256), BF16),
            pltpu.VMEM((NB, 4, 32, 256), BF16),
            pltpu.VMEM((NB, 4, 32, 256), BF16),
            pltpu.VMEM((NB, 3, 32, 256), BF16),
            pltpu.VMEM((NB, 3, 32, 256), BF16),
            pltpu.VMEM((4, 8, NB * 512), F32),
            pltpu.VMEM((3, 8, NB * 512), F32),
            *gather_sems(), *gather_sems(), *gather_sems(),
            dma((NB,)), dma((NB,)), dma((NB, 6)), dma((NB, 6)), dma((NB, 6)), dma((NB, 6)),
            dma((3,)), dma((3,)),
        ],
        compiler_params=pltpu.CompilerParams(
            collective_id=0, has_side_effects=True, vmem_limit_bytes=67043328),
    )(tokens_in[0], user_ids, w_in, w_out, cotangent[0])
    return output[None], grad_tokens[None], total_in, total_out.T


def solution(mesh):
    in_specs = (P("dp", "seq", None), P("dp", None), P(), P(), P("dp", "seq", None))
    out_specs = (
        P("dp", "seq", None),
        P("dp", "seq", None),
        P(("dp", "seq"), None),
        P(None, ("dp", "seq")),
    )
    return jax.shard_map(local, mesh=mesh, in_specs=in_specs, out_specs=out_specs, check_vma=False)
```

```python
import math

import jax
import jax.numpy as jnp
from jax import lax
from jax.experimental import pallas as pl
from jax.experimental.pallas import tpu as pltpu
from jax.sharding import PartitionSpec as P

HEADS = 4
HD = 128
ROWS = 512
F32 = jnp.float32
BF16 = jnp.bfloat16
EPS = 1e-05
HALF_SCALE = 0.5 / math.sqrt(HD)
MESH = pl.DeviceIdType.MESH
NB = 5

OWN_MOVES = (
    (0, 1, 0, (0, 1, 2, 3)),
    (0, 3, 0, (2, 3)),
    (1, 2, 1, (0, 1, 2)),
    (1, 0, 1, (3, 1, 2)),
    (2, 3, 2, (0, 1, 2, 3)),
)
RELAYS = {
    (1, 0, 0): 2, (1, 0, 1): 2,
    (0, 1, 3): 3, (0, 1, 1): 3, (0, 1, 2): 3,
    (3, 0, 2): 2, (3, 0, 3): 2, (3, 1, 3): 2,
    (2, 1, 0): 3,
}
ARRIVALS = {
    0: ((1, 3), (1, 1), (1, 2)),
    1: ((0, 0), (0, 1), (0, 2), (0, 3)),
    2: ((1, 0), (1, 1), (0, 2), (1, 2), (0, 3), (0, 0), (1, 3), (0, 1)),
    3: ((2, 0), (0, 2), (2, 1), (0, 3), (2, 2), (1, 3), (2, 3), (1, 1), (1, 2), (1, 0)),
}
STEPS = 10
QUERY_MOVES = (
    (0, 1, 0, (0, 1)),
    (0, 3, 0, (2, 3)),
    (1, 2, 1, (0, 1, 2, 3)),
    (2, 3, 2, (0, 1, 2, 3)),
    (1, 0, 1, (3, 2)),
    (0, 1, 0, (2, 3)),
)
QUERY_RELAYS = {
    (1, 0, 0): 2, (1, 0, 1): 2,
    (3, 0, 2): 2, (3, 0, 3): 2,
    (2, 1, 0): 3, (2, 1, 1): 3,
    (0, 1, 3): 3, (0, 1, 2): 3,
}
QUERY_ARRIVALS = {
    0: ((1, 3), (1, 2)),
    1: ((0, 0), (0, 1), (0, 2), (0, 3)),
    2: ((1, 0), (1, 1), (1, 2), (1, 3), (0, 2), (0, 3), (0, 0), (0, 1)),
    3: ((0, 2), (0, 3), (2, 0), (2, 1), (2, 2), (2, 3), (1, 0), (1, 1), (1, 3), (1, 2)),
}
GRAD_ARRIVALS = {
    0: ((1, 3), (1, 1), (1, 2)),
    1: ((0, 0), (0, 1), (0, 2), (0, 3)),
    2: ((1, 0), (1, 1), (0, 2), (1, 2), (0, 0), (0, 3), (0, 1), (1, 3)),
    3: ((2, 0), (2, 1), (0, 2), (2, 2), (0, 3), (2, 3), (1, 3), (1, 1), (1, 0), (1, 2)),
}


def place():
    dp, seq = lax.axis_index("dp"), lax.axis_index("seq")
    return dp // 4, dp % 4, seq // 2, seq % 2


def device(y, x, z, core):
    return {"dp": y * 4 + x, "seq": z * 2 + core}


def turn(i, d):
    return lax.rem(i + d, 4)


def remote(src, dst, send, recv, target):
    return pltpu.make_async_remote_copy(
        src_ref=src, dst_ref=dst, send_sem=send, recv_sem=recv,
        device_id=target, device_id_type=MESH)


def dot_nn(a, b):
    return jnp.dot(a, b, preferred_element_type=F32)


def dot_nt(a, b):
    return lax.dot_general(a, b, (((1,), (1,)), ((), ())), preferred_element_type=F32)


def dot_tn(a, b):
    return lax.dot_general(a, b, (((0,), (0,)), ((), ())), preferred_element_type=F32)


class Gather:
    def __init__(self, buf, sems, chip, core, target, moves, relays, arrivals):
        self.buf, self.near, self.far = buf, buf.at[0], buf.at[1]
        self.ss, self.rs, self.sp, self.rp = sems
        self.chip, self.core, self.target = chip, core, target
        self.moves, self.relays, self.arrivals = moves, relays, arrivals

    def move(self, sender, receiver, owner, h):
        k = 0 if receiver == sender + 1 else 1
        return remote(self.near.at[owner, h], self.near.at[owner, h], self.ss.at[owner, h, k],
                      self.rs.at[owner, h], self.target(receiver, self.core))

    def share(self, owner, h):
        return remote(self.near.at[owner, h], self.far.at[owner, h], self.sp.at[owner, h],
                      self.rp.at[owner, h], self.target(self.chip, 1 - self.core))

    def start(self, moves=None, share=True):
        if share:
            @pl.when(self.core == 0)
            def _():
                for h in range(HEADS):
                    self.share(self.chip, h).start()
        for sender, receiver, owner, heads in (self.moves if moves is None else moves):
            @pl.when(self.chip == sender)
            def _():
                for h in heads:
                    self.move(sender, receiver, owner, h).start()

    def arrive(self, step, roles=(0, 1, 2, 3)):
        for role in roles:
            order = self.arrivals.get(role, ())
            if step >= len(order):
                continue
            owner, h = order[step]

            @pl.when(self.chip == role)
            def _():
                self.move(role, (role + 1) % 4, owner, h).wait_recv()
                if (role, owner, h) in self.relays:
                    self.move(role, self.relays[role, owner, h], owner, h).start()
                if owner == role - 1:
                    self.share(owner, h).start()
                if owner == role - 2:
                    @pl.when(self.core == 1)
                    def _():
                        self.share(owner, h).start()

    def look(self, step):
        code = jnp.int32(-1)
        for role, order in self.arrivals.items():
            for k, (owner, h) in enumerate(order):
                value = (self.relays.get((role, owner, h), -1) + 1) * 16 + owner * 4 + h
                code = jnp.where((self.chip == role) & (step == k), value, code)
        return code >= 0, (code // 4) % 4, code % 4, code // 16 - 1

    def service(self, step, serve=None):
        wanted, owner, h, dest = self.look(step)
        if serve is not None:
            wanted = wanted & serve

        @pl.when(wanted)
        def _():
            here = self.near.at[owner, h]
            gap = self.chip - owner
            remote(here, here, self.ss.at[owner, h, 0], self.rs.at[owner, h],
                   self.target(turn(self.chip, 1), self.core)).wait_recv()

            @pl.when(dest >= 0)
            def _():
                k = jnp.where(dest == self.chip + 1, 0, 1)
                remote(here, here, self.ss.at[owner, h, k], self.rs.at[owner, h],
                       self.target(dest, self.core)).start()

            @pl.when((gap == 1) | ((gap == 2) & (self.core == 1)))
            def _():
                self.share(owner, h).start()

    def drain(self):
        @pl.when(self.core == 0)
        def _():
            for h in range(HEADS):
                self.share(self.chip, h).wait_send()
        for sender, receiver, owner, heads in self.moves:
            @pl.when(self.chip == sender)
            def _():
                for h in heads:
                    self.move(sender, receiver, owner, h).wait_send()
        for (role, owner, h), receiver in self.relays.items():
            @pl.when(self.chip == role)
            def _():
                self.move(role, receiver, owner, h).wait_send()
        for role, order in self.arrivals.items():
            for owner, h in order:
                if owner == role - 1:
                    @pl.when(self.chip == role)
                    def _():
                        self.share(owner, h).wait_send()
                if owner == role - 2:
                    @pl.when((self.chip == role) & (self.core == 1))
                    def _():
                        self.share(owner, h).wait_send()


def layer_kernel(tokens_hbm, ids, w_in_hbm, w_out_hbm, cot_hbm, output_hbm, grad_tokens_hbm, out_in, out_out,
                 output, grad_tokens, out_sems, tokens, w_in, w_out, cot, in_sems, normed_t, cot_t, normed, slope, u, kv, qs, gs, att, dq, dk, dv, gated, gh, masks, masks_t,
                 tmp, part, s2, recv1, r2a, r2b, s3a, s3b, r3a, r3b, t4, r4,
                 kss, krs, ksp, krp, qss, qrs, qsp, qrp, gss, grs, gsp, grp,
                 ss1, rs1, ss2, rs2, ss3, rs3, ss4, rs4):
    y, x, z, c = place()
    other = 1 - c
    block = z * 2 + c
    peers = ([device(y, x, z, other)]
             + [device(y, turn(x, d), z, c) for d in (1, 2, 3)]
             + [device(turn(y, d), x, z, c) for d in (1, 2, 3)]
             + [device(y, x, turn(z, d), c) for d in (1, 2, 3)])
    barrier = pltpu.get_barrier_semaphore()
    for t in peers:
        pl.semaphore_signal(barrier, inc=1, device_id=t, device_id_type=MESH)

    tokens_in = pltpu.make_async_copy(tokens_hbm, tokens, in_sems.at[0])
    tokens_in.start()
    w_ins = {}
    for i, col in enumerate((1536, 512, 1024, 0)):
        cols = pl.ds(col, 512)
        w_ins[col] = pltpu.make_async_copy(w_in_hbm.at[:, cols], w_in.at[:, cols], in_sems.at[1 + i])
        w_ins[col].start()
    cot_in = pltpu.make_async_copy(cot_hbm, cot, in_sems.at[5])
    w_out_in = pltpu.make_async_copy(w_out_hbm, w_out, in_sems.at[6])
    cot_in.start()
    w_out_in.start()
    mz, mc = 3 - z, 1 - c

    def mirrored(zz, cc):
        return device(y, x, 3 - zz, 1 - cc)

    before = Gather(kv, (kss, krs, ksp, krp), z, c, lambda zz, cc: device(y, x, zz, cc),
                    OWN_MOVES, RELAYS, ARRIVALS)
    queries = Gather(qs, (qss, qrs, qsp, qrp), mz, mc, mirrored,
                     QUERY_MOVES, QUERY_RELAYS, QUERY_ARRIVALS)
    grads = Gather(gs, (gss, grs, gsp, grp), mz, mc, mirrored,
                   OWN_MOVES, RELAYS, GRAD_ARRIVALS)

    def stats(v):
        center = v - jnp.mean(v, axis=-1, keepdims=True)
        inverse = lax.rsqrt(jnp.mean(center * center, axis=-1, keepdims=True) + EPS)
        return center * inverse, inverse

    def row_loop(size):
        def wrap(body):
            @pl.loop(0, ROWS // size)
            def _(i):
                body(pl.ds(pl.multiple_of(i * size, size), size))
        return wrap

    tokens_in.wait()

    @row_loop(128)
    def _(rows):
        normed[rows, :] = stats(tokens[rows, :].astype(F32))[0].astype(BF16)

    def features(col, put):
        w_ins[col].wait()

        @row_loop(256)
        def _(rows):
            half = 0.5 * dot_nn(normed[rows, :], w_in[:, col:col + 512])
            t = jnp.tanh(half)
            slope[rows, col:col + 512] = 0.5 * (1.0 + t) * (1.0 + half * (1.0 - t))
            put(rows, (half * (1.0 + t)).astype(BF16))

    def put_k(rows, a):
        for h in range(HEADS):
            kv[0, z, h, rows, 0:128] = a[:, h * 128:(h + 1) * 128]

    def put_v(rows, a):
        for h in range(HEADS):
            kv[0, z, h, rows, 128:256] = a[:, h * 128:(h + 1) * 128]

    def put_q(rows, a):
        for h in range(HEADS):
            qs[0, mz, h, rows, :] = a[:, h * 128:(h + 1) * 128]

    def put_u(rows, a):
        u[rows, :] = a

    features(1536, put_k)
    features(512, put_v)
    pl.semaphore_wait(barrier, len(peers))
    before.start()
    features(1024, put_q)
    queries.start(QUERY_MOVES[:4])
    features(0, put_u)

    def ids_of(b):
        b = jnp.clip(b, 0, 7)
        return ids[:, pl.ds(pl.multiple_of(b * ROWS, ROWS), ROWS)].astype(F32)

    own_ids = jnp.transpose(jnp.broadcast_to(ids_of(block), (128, ROWS)))
    own_col = jnp.broadcast_to(own_ids[:, 0:1], (ROWS, ROWS))
    one, nil = jnp.ones((ROWS, ROWS), F32), jnp.zeros((ROWS, ROWS), F32)
    down = lax.broadcasted_iota(jnp.int32, (ROWS, ROWS), 0)
    right = lax.broadcasted_iota(jnp.int32, (ROWS, ROWS), 1)
    for d in range(5):
        same = own_col == jnp.broadcast_to(ids_of(block - d), (ROWS, ROWS))
        same_t = own_col == jnp.broadcast_to(ids_of(block + d), (ROWS, ROWS))
        if d == 0:
            same = same & (right <= down)
            same_t = same_t & (down <= right)
        masks[d] = jnp.where(same, one, nil).astype(BF16)
        masks_t[d] = jnp.where(same_t, one, nil).astype(BF16)

    def pipeline(items, scores, weigh, add):
        ahead = scores(*items[0])
        for i, item in enumerate(items):
            now = ahead
            if i + 1 < len(items):
                ahead = scores(*items[i + 1])
            add(item, weigh(now, item))

    def tiles(where, flip, heads, d):
        out = []
        for h in heads:
            for r in (0, 256):
                cols = (0, 512)
                if isinstance(d, int) and d == 0:
                    cols = ((0, 256), (0, 512))[r // 256] if not flip else ((0, 512), (256, 512))[r // 256]
                out.append(where + (h, d, (r, r + 256), cols))
        return out

    def forward_tiles(items, first=False):
        def scores(e, o, h, d, rows, cols):
            return dot_nt(qs[0, mz, h, rows[0]:rows[1], :], kv[e, o, h, cols[0]:cols[1], 0:128])

        def weigh(now, item):
            e, o, h, d, rows, cols = item
            half = (now * HALF_SCALE).astype(BF16)
            return (half + half * jnp.tanh(half)) * masks[d, rows[0]:rows[1], cols[0]:cols[1]]

        def add(item, w):
            e, o, h, d, rows, cols = item
            a = dot_nn(w, kv[e, o, h, cols[0]:cols[1], 128:256])
            if first:
                att[h, rows[0]:rows[1], :] = a
            else:
                att[h, rows[0]:rows[1], :] += a

        pipeline(items, scores, weigh, add)

    def query_tiles(items, first=False):
        def scores(e, o, h, d, rows, cols):
            keys = slice(cols[0], cols[1])
            mine = slice(rows[0], rows[1])
            return (dot_nt(qs[0, mz, h, mine, :], kv[e, o, h, keys, 0:128]),
                    dot_nt(gs[0, mz, h, mine, :], kv[e, o, h, keys, 128:256]))

        def weigh(now, item):
            e, o, h, d, rows, cols = item
            half = (now[0] * HALF_SCALE).astype(BF16)
            t = jnp.tanh(half)
            a = (t + 1) * masks[d, rows[0]:rows[1], cols[0]:cols[1]]
            return now[1].astype(BF16) * (a + half * a * (1 - t))

        def add(item, ds):
            e, o, h, d, rows, cols = item
            a = dot_nn(ds, kv[e, o, h, cols[0]:cols[1], 0:128])
            if first:
                dq[h, rows[0]:rows[1], :] = a
            else:
                dq[h, rows[0]:rows[1], :] += a

        pipeline(items, scores, weigh, add)

    def key_tiles(items, first=False):
        def scores(e, o, h, d, rows, cols):
            theirs = slice(cols[0], cols[1])
            mine = slice(rows[0], rows[1])
            return (dot_nt(kv[0, z, h, mine, 0:128], qs[e, o, h, theirs, :]),
                    dot_nt(kv[0, z, h, mine, 128:256], gs[e, o, h, theirs, :]))

        def weigh(now, item):
            e, o, h, d, rows, cols = item
            half = (now[0] * HALF_SCALE).astype(BF16)
            t = jnp.tanh(half)
            a = (t + 1) * masks_t[d, rows[0]:rows[1], cols[0]:cols[1]]
            w = half * a
            return w, now[1].astype(BF16) * (a + w * (1 - t))

        def add(item, got):
            e, o, h, d, rows, cols = item
            av = dot_nn(got[0], gs[e, o, h, cols[0]:cols[1], :])
            ak = dot_nn(got[1], qs[e, o, h, cols[0]:cols[1], :])
            if first:
                dv[h, rows[0]:rows[1], :] = av
                dk[h, rows[0]:rows[1], :] = ak
            else:
                dv[h, rows[0]:rows[1], :] += av
                dk[h, rows[0]:rows[1], :] += ak

        pipeline(items, scores, weigh, add)

    def meet(gather, step, compute, flip, also=None):
        there, o, h, _ = gather.look(step)
        gap = gather.chip - o
        even = 2 * gap
        odd = even + 2 * gather.core - 1

        @pl.when(there & ((gap == 1) | ((gap == 2) & (gather.core == 0))))
        def _():
            gather.share(o, h).wait_recv()
            if also is not None:
                also.share(o, h).wait_recv()
            compute(tiles((0, o), flip, (h,), even) + tiles((1, o), flip, (h,), odd))

        @pl.when(there & (gap == 2) & (gather.core == 1))
        def _():
            compute(tiles((0, o), flip, (h,), even))

    def beside(gather, compute, flip, also=None):
        @pl.when(gather.core == 1)
        def _():
            @pl.loop(0, 2)
            def _(pair):
                heads = (2 * pair, 2 * pair + 1)
                for h in heads:
                    gather.share(gather.chip, h).wait_recv()
                    if also is not None:
                        also.share(gather.chip, h).wait_recv()
                compute(tiles((1, gather.chip), flip, heads, 1))

    def pair_copy(b):
        return remote(s2.at[b], recv1.at[b], ss1.at[b], rs1.at[b], device(y, x, z, other))

    def weight(b, left, cols):
        @pl.loop(0, 4)
        def _(r):
            rows = pl.ds(pl.multiple_of(r * 256, 256), 256)
            tmp[...] = dot_nn(left[rows, :], cols).reshape(16, 2, 8, 512)
            half = pl.ds(pl.multiple_of(r * 128, 128), 128)
            part[b, half, :] = tmp[:, c].reshape(128, 512)
            s2[b, r] = tmp[:, other].reshape(4, 32, 512).astype(BF16)
        pair_copy(b).start()

    def plane_copies(b):
        out = []
        for d in (1, 2, 3):
            xx, yy = turn(x, d), turn(y, d)
            out.append(remote(s2.at[b, :, xx, :, pl.ds(0, 256)], r2a.at[b, d - 1], ss2.at[b, d - 1],
                              rs2.at[b, d - 1], device(y, xx, z, c)))
            out.append(remote(s2.at[b, yy, :, :, pl.ds(256, 256)], r2b.at[b, d - 1], ss2.at[b, d + 2],
                              rs2.at[b, d + 2], device(yy, x, z, c)))
        return out

    def line_copies(b):
        out = []
        for d in (1, 2, 3):
            xx, yy = turn(x, d), turn(y, d)
            out.append(remote(s3a.at[b, yy], r3a.at[b, d - 1], ss3.at[b, d - 1], rs3.at[b, d - 1],
                              device(yy, x, z, c)))
            out.append(remote(s3b.at[b, xx], r3b.at[b, d - 1], ss3.at[b, d + 2], rs3.at[b, d + 2],
                              device(y, xx, z, c)))
        return out

    def second(b):
        pair_copy(b).wait()
        for i in range(4):
            mine = part[b, i * 128:(i + 1) * 128, :].reshape(4, 32, 512)
            s2[b, i] = (mine + recv1[b, i].astype(F32)).astype(BF16)
        for cp in plane_copies(b):
            cp.start()

    def third(b):
        for cp in plane_copies(b):
            cp.wait()
        a = s2[b, :, x, :, 0:256].astype(F32)
        e = s2[b, y, :, :, 256:512].astype(F32)
        for d in range(3):
            a = a + r2a[b, d].astype(F32)
            e = e + r2b[b, d].astype(F32)
        s3a[b] = a.astype(BF16)
        s3b[b] = e.astype(BF16)
        for cp in line_copies(b):
            cp.start()

    def fourth(b):
        for cp in line_copies(b):
            cp.wait()
        a = s3a[b, y].astype(F32)
        e = s3b[b, x].astype(F32)
        for d in range(3):
            a = a + r3a[b, d].astype(F32)
            e = e + r3b[b, d].astype(F32)
        t4[:, :, b * 512:b * 512 + 256] = a.reshape(4, 8, 256)
        t4[:, :, b * 512 + 256:b * 512 + 512] = e.reshape(4, 8, 256)

    forward_tiles(tiles((0, z), False, range(HEADS), 0), first=True)
    cot_in.wait()
    w_out_in.wait()

    @row_loop(128)
    def _(rows):
        normed_t[:, rows] = jnp.transpose(normed[rows, :])
        cot_t[:, rows] = jnp.transpose(cot[rows, :])

    beside(before, forward_tiles, False)
    before.service(0)
    before.service(1)
    queries.start(QUERY_MOVES[4:5], share=False)
    for step in range(2):
        queries.arrive(step, roles=(1, 2, 3))

    @pl.loop(0, STEPS)
    def _(step):
        meet(before, step, forward_tiles, False)
        before.service(step + 2)

        @pl.when(step == 3)
        def _():
            queries.start(QUERY_MOVES[5:], share=False)


    @row_loop(256)
    def _(rows):
        a = jnp.concatenate([att[h, rows, :] for h in range(HEADS)], axis=1)
        no, inverse = stats(a)
        uu = u[rows, :].astype(F32)
        g = (no * uu).astype(BF16)
        gated[rows, :] = g
        output[rows, :] = (dot_nn(g, w_out[...]) + tokens[rows, :].astype(F32)).astype(BF16)
        gg = dot_nt(cot[rows, :], w_out[...])
        gh[rows, 0:512] = (gg * no * slope[rows, 0:512]).astype(BF16)
        gn = gg * uu
        back = inverse * (gn - jnp.mean(gn, axis=-1, keepdims=True)
                          - no * jnp.mean(gn * no, axis=-1, keepdims=True))
        back = back.astype(BF16)
        for h in range(HEADS):
            gs[0, mz, h, rows, :] = back[:, h * 128:(h + 1) * 128]

    grads.start()
    output_out = pltpu.make_async_copy(output, output_hbm, out_sems.at[0])
    output_out.start()
    query_tiles(tiles((0, z), False, range(HEADS), 0), first=True)
    weight(0, cot_t, gated[...])
    weight(1, normed_t, gh[:, 0:512])
    queries.arrive(0, roles=(0,))
    queries.arrive(1, roles=(0,))
    queries.arrive(2, roles=(1,))
    early = mz < 2

    @pl.loop(1, 5)
    def _(d):
        grads.service(d - 1, serve=early)

        @pl.when(block >= d)
        def _():
            owner = jnp.where(d % 2 == 0, z - d // 2, z - (d + 1) // 2 + c)
            query_tiles(tiles((d % 2, owner), False, range(HEADS), d))

    second(0)
    second(1)
    queries.arrive(3, roles=(1,))

    @row_loop(256)
    def _(rows):
        for h in range(HEADS):
            at = 1024 + h * 128
            gh[rows, at:at + 128] = (dq[h, rows, :] * HALF_SCALE * slope[rows, at:at + 128]).astype(BF16)

    weight(3, normed_t, gh[:, 1024:1536])
    key_tiles(tiles((0, mz), True, range(HEADS), 0), first=True)
    beside(grads, key_tiles, True, also=queries)
    second(3)
    third(0)
    third(1)
    late = mz >= 2
    grads.service(0, serve=late)
    for step in range(2, 8):
        queries.arrive(step, roles=(2,))
    for step in range(2, STEPS):
        queries.arrive(step, roles=(3,))

    @pl.loop(0, STEPS)
    def _(step):
        grads.service(step + 1, serve=late)
        meet(grads, step, key_tiles, True, also=queries)

    @row_loop(256)
    def _(rows):
        for h in range(HEADS):
            at = 512 + h * 128
            gh[rows, at:at + 128] = (dv[h, rows, :] * slope[rows, at:at + 128]).astype(BF16)
            at = 1536 + h * 128
            gh[rows, at:at + 128] = (dk[h, rows, :] * HALF_SCALE * slope[rows, at:at + 128]).astype(BF16)

    weight(2, normed_t, gh[:, 512:1024])
    weight(4, normed_t, gh[:, 1536:2048])
    third(3)
    second(2)
    second(4)

    @row_loop(256)
    def _(rows):
        up = dot_nt(gh[rows, :], w_in[...])
        zhat, inverse = stats(tokens[rows, :].astype(F32))
        back = inverse * (up - jnp.mean(up, axis=-1, keepdims=True)
                          - zhat * jnp.mean(up * zhat, axis=-1, keepdims=True))
        grad_tokens[rows, :] = (back + cot[rows, :].astype(F32)).astype(BF16)

    tokens_out = pltpu.make_async_copy(grad_tokens, grad_tokens_hbm, out_sems.at[1])
    tokens_out.start()
    fourth(0)
    fourth(1)
    fourth(3)
    third(2)
    third(4)
    fourth(2)
    fourth(4)
    last = []
    for d in (1, 2, 3):
        zz = turn(z, d)
        cp = remote(t4.at[zz], r4.at[d - 1], ss4.at[d - 1], rs4.at[d - 1], device(y, x, zz, c))
        cp.start()
        last.append(cp)
    before.drain()
    queries.drain()
    grads.drain()
    output_out.wait()
    tokens_out.wait()
    for cp in last:
        cp.wait()
    total = t4[z] + r4[0] + r4[1] + r4[2]
    out_out[...] = total[:, 0:512]
    out_in[...] = total[:, 512:2560]


def finish_kernel(a, b, p, q, out_a, out_b, out_p, out_q, va, vb, vp, vq, ins, outs):
    moves = []
    for i in range(4):
        rows = pl.ds(i * 128, 128)
        moves.append((a.at[rows, :], va.at[rows, :], out_a.at[0, rows, :]))
        moves.append((b.at[rows, :], vb.at[rows, :], out_b.at[0, rows, :]))
    moves.append((p, vp, out_p))
    fetch = [pltpu.make_async_copy(q, vq, ins.at[9])]
    fetch += [pltpu.make_async_copy(src, mid, ins.at[i]) for i, (src, mid, _) in enumerate(moves)]
    store = [pltpu.make_async_copy(mid, dst, outs.at[i]) for i, (_, mid, dst) in enumerate(moves)]
    last = pltpu.make_async_copy(vq, out_q, outs.at[9])
    for cp in fetch:
        cp.start()
    fetch[0].wait()
    last.start()
    for got, put in zip(fetch[1:], store):
        got.wait()
        put.start()
    for put in store:
        put.wait()
    last.wait()


def finish(output, grad_tokens, total_in, total_out):
    hbm = pl.BlockSpec(memory_space=pl.ANY)
    dma = pltpu.SemaphoreType.DMA
    return pl.pallas_call(
        finish_kernel,
        name="finish",
        out_shape=(
            jax.ShapeDtypeStruct((1, ROWS, 1024), BF16),
            jax.ShapeDtypeStruct((1, ROWS, 1024), BF16),
            jax.ShapeDtypeStruct((8, 2048), F32),
            jax.ShapeDtypeStruct((8, 512), F32),
        ),
        in_specs=[hbm] * 4,
        out_specs=(hbm,) * 4,
        scratch_shapes=[
            pltpu.VMEM((ROWS, 1024), BF16),
            pltpu.VMEM((ROWS, 1024), BF16),
            pltpu.VMEM((8, 2048), F32),
            pltpu.VMEM((8, 512), F32),
            dma((10,)), dma((10,)),
        ],
    )(output, grad_tokens, total_in, total_out)


def local(tokens_in, user_ids, w_in, w_out, cotangent):
    vmem = pl.BlockSpec(memory_space=pltpu.VMEM)
    hbm = pl.BlockSpec(memory_space=pl.ANY)
    dma = pltpu.SemaphoreType.DMA

    def gather_sems():
        return [dma((4, 4, 2)), dma((4, 4)), dma((4, 4)), dma((4, 4))]

    output, grad_tokens, total_in, total_out = pl.pallas_call(
        layer_kernel,
        name="layer",
        out_shape=(
            jax.ShapeDtypeStruct((ROWS, 1024), BF16),
            jax.ShapeDtypeStruct((ROWS, 1024), BF16),
            jax.ShapeDtypeStruct((8, 2048), F32),
            jax.ShapeDtypeStruct((8, 512), F32),
        ),
        in_specs=[hbm, vmem, hbm, hbm, hbm],
        out_specs=(hbm, hbm, vmem, vmem),
        scratch_shapes=[
            pltpu.VMEM((ROWS, 1024), BF16),
            pltpu.VMEM((ROWS, 1024), BF16),
            dma((2,)),
            pltpu.VMEM((ROWS, 1024), BF16),
            pltpu.VMEM((1024, 2048), BF16),
            pltpu.VMEM((512, 1024), BF16),
            pltpu.VMEM((ROWS, 1024), BF16),
            dma((7,)),
            pltpu.VMEM((1024, ROWS), BF16),
            pltpu.VMEM((1024, ROWS), BF16),
            pltpu.VMEM((ROWS, 1024), BF16),
            pltpu.VMEM((ROWS, 2048), F32),
            pltpu.VMEM((ROWS, 512), BF16),
            pltpu.VMEM((2, 4, 4, ROWS, 256), BF16),
            pltpu.VMEM((2, 4, 4, ROWS, 128), BF16),
            pltpu.VMEM((2, 4, 4, ROWS, 128), BF16),
            pltpu.VMEM((4, ROWS, 128), F32),
            pltpu.VMEM((4, ROWS, 128), F32),
            pltpu.VMEM((4, ROWS, 128), F32),
            pltpu.VMEM((4, ROWS, 128), F32),
            pltpu.VMEM((ROWS, 512), BF16),
            pltpu.VMEM((ROWS, 2048), BF16),
            pltpu.VMEM((5, ROWS, ROWS), BF16),
            pltpu.VMEM((5, ROWS, ROWS), BF16),
            pltpu.VMEM((16, 2, 8, 512), F32),
            pltpu.VMEM((NB, 512, 512), F32),
            pltpu.VMEM((NB, 4, 4, 32, 512), BF16),
            pltpu.VMEM((NB, 4, 4, 32, 512), BF16),
            pltpu.VMEM((NB, 3, 4, 32, 256), BF16),
            pltpu.VMEM((NB, 3, 4, 32, 256), BF16),
            pltpu.VMEM((NB, 4, 32, 256), BF16),
            pltpu.VMEM((NB, 4, 32, 256), BF16),
            pltpu.VMEM((NB, 3, 32, 256), BF16),
            pltpu.VMEM((NB, 3, 32, 256), BF16),
            pltpu.VMEM((4, 8, NB * 512), F32),
            pltpu.VMEM((3, 8, NB * 512), F32),
            *gather_sems(), *gather_sems(), *gather_sems(),
            dma((NB,)), dma((NB,)), dma((NB, 6)), dma((NB, 6)), dma((NB, 6)), dma((NB, 6)),
            dma((3,)), dma((3,)),
        ],
        compiler_params=pltpu.CompilerParams(
            collective_id=0, has_side_effects=True, vmem_limit_bytes=67043328),
    )(tokens_in[0], user_ids, w_in, w_out, cotangent[0])
    output, grad_tokens, total_in, total_out = finish(output, grad_tokens, total_in, total_out)
    return output, grad_tokens, total_in, total_out.T


def solution(mesh):
    in_specs = (P("dp", "seq", None), P("dp", None), P(), P(), P("dp", "seq", None))
    out_specs = (
        P("dp", "seq", None),
        P("dp", "seq", None),
        P(("dp", "seq"), None),
        P(None, ("dp", "seq")),
    )
    return jax.shard_map(local, mesh=mesh, in_specs=in_specs, out_specs=out_specs, check_vma=False)
```

```python
import math

import jax
import jax.numpy as jnp
from jax import lax
from jax.experimental import pallas as pl
from jax.experimental.pallas import tpu as pltpu
from jax.sharding import PartitionSpec as P

HEADS = 4
HD = 128
ROWS = 512
F32 = jnp.float32
BF16 = jnp.bfloat16
EPS = 1e-05
HALF_SCALE = 0.5 / math.sqrt(HD)
MESH = pl.DeviceIdType.MESH
NB = 5
GROUPS = ((0, 2), (2, 1), (3, 2))

OWN_MOVES = (
    (0, 1, 0, (0, 1, 2, 3)),
    (0, 3, 0, (0, 1)),
    (1, 2, 1, (1, 2, 3)),
    (1, 0, 1, (0, 1, 2)),
    (2, 3, 2, (0, 1, 2, 3)),
)
RELAYS = {
    (1, 0, 2): 2, (1, 0, 3): 2,
    (0, 1, 0): 3, (0, 1, 1): 3, (0, 1, 2): 3,
    (3, 0, 0): 2, (3, 0, 1): 2, (3, 1, 0): 2,
    (2, 1, 3): 3,
}
ARRIVALS = {
    0: ((1, 0), (1, 1), (1, 2)),
    1: ((0, 0), (0, 1), (0, 2), (0, 3)),
    2: ((1, 1), (0, 0), (1, 2), (0, 1), (1, 3), (1, 0), (0, 2), (0, 3)),
    3: ((2, 0), (0, 0), (2, 1), (0, 1), (2, 2), (1, 0), (2, 3), (1, 1), (1, 2), (1, 3)),
}
STEPS = 10
QUERY_MOVES = (
    (0, 1, 0, (0, 1)),
    (0, 3, 0, (2, 3)),
    (1, 2, 1, (0, 1, 2, 3)),
    (2, 3, 2, (0, 1, 2, 3)),
    (1, 0, 1, (3, 2)),
    (0, 1, 0, (2, 3)),
)
QUERY_RELAYS = {
    (1, 0, 0): 2, (1, 0, 1): 2,
    (3, 0, 2): 2, (3, 0, 3): 2,
    (2, 1, 0): 3, (2, 1, 1): 3,
    (0, 1, 3): 3, (0, 1, 2): 3,
}
QUERY_ARRIVALS = {
    0: ((1, 3), (1, 2)),
    1: ((0, 0), (0, 1), (0, 2), (0, 3)),
    2: ((1, 0), (1, 1), (1, 2), (1, 3), (0, 2), (0, 3), (0, 0), (0, 1)),
    3: ((0, 2), (0, 3), (2, 0), (2, 1), (2, 2), (2, 3), (1, 0), (1, 1), (1, 3), (1, 2)),
}
GRAD_ARRIVALS = {
    0: ((1, 0), (1, 1), (1, 2)),
    1: ((0, 0), (0, 1), (0, 2), (0, 3)),
    2: ((1, 1), (1, 2), (0, 0), (1, 3), (0, 2), (0, 1), (0, 3), (1, 0)),
    3: ((2, 0), (2, 1), (0, 0), (2, 2), (0, 1), (2, 3), (1, 0), (1, 1), (1, 3), (1, 2)),
}


def place():
    dp, seq = lax.axis_index("dp"), lax.axis_index("seq")
    return dp // 4, dp % 4, seq // 2, seq % 2


def device(y, x, z, core):
    return {"dp": y * 4 + x, "seq": z * 2 + core}


def turn(i, d):
    return lax.rem(i + d, 4)


def remote(src, dst, send, recv, target):
    return pltpu.make_async_remote_copy(
        src_ref=src, dst_ref=dst, send_sem=send, recv_sem=recv,
        device_id=target, device_id_type=MESH)


def dot_nn(a, b):
    return jnp.dot(a, b, preferred_element_type=F32)


def dot_nt(a, b):
    return lax.dot_general(a, b, (((1,), (1,)), ((), ())), preferred_element_type=F32)


def dot_tn(a, b):
    return lax.dot_general(a, b, (((0,), (0,)), ((), ())), preferred_element_type=F32)


class Gather:
    def __init__(self, buf, sems, chip, core, target, moves, relays, arrivals):
        self.buf, self.near, self.far = buf, buf.at[0], buf.at[1]
        self.ss, self.rs, self.sp, self.rp = sems
        self.chip, self.core, self.target = chip, core, target
        self.moves, self.relays, self.arrivals = moves, relays, arrivals
        self.sent = {}
        for role in range(4):
            mine = [(receiver, owner, h) for sender, receiver, owner, heads in moves if sender == role for h in heads]
            mine += [(receiver, owner, h) for (sender, owner, h), receiver in relays.items() if sender == role]
            for k, (receiver, owner, h) in enumerate(mine):
                self.sent[role, receiver, owner, h] = k

    def move(self, sender, receiver, owner, h):
        return remote(self.near.at[owner, h], self.near.at[owner, h], self.ss.at[self.sent[sender, receiver, owner, h]],
                      self.rs.at[self.arrivals[receiver].index((owner, h))], self.target(receiver, self.core))

    def landed(self, step, owner, h):
        here = self.near.at[owner, h]
        return remote(here, here, self.ss.at[0], self.rs.at[step], self.target(turn(self.chip, 1), self.core))

    def share(self, owner, h):
        k = jnp.where(self.chip - owner == 1, 4, 0) + h
        return remote(self.near.at[owner, h], self.far.at[owner, h], self.sp.at[k],
                      self.rp.at[k], self.target(self.chip, 1 - self.core))

    def start(self, moves=None, share=True, only=(0, 1, 2, 3)):
        if share:
            @pl.when(self.core == 0)
            def _():
                for h in only:
                    self.share(self.chip, h).start()
        for sender, receiver, owner, heads in (self.moves if moves is None else moves):
            @pl.when(self.chip == sender)
            def _():
                for h in heads:
                    if h in only:
                        self.move(sender, receiver, owner, h).start()

    def arrive(self, step, roles=(0, 1, 2, 3)):
        for role in roles:
            order = self.arrivals.get(role, ())
            if step >= len(order):
                continue
            owner, h = order[step]

            @pl.when(self.chip == role)
            def _():
                self.landed(step, owner, h).wait_recv()
                if (role, owner, h) in self.relays:
                    self.move(role, self.relays[role, owner, h], owner, h).start()
                if owner == role - 1:
                    self.share(owner, h).start()
                if owner == role - 2:
                    @pl.when(self.core == 1)
                    def _():
                        self.share(owner, h).start()

    def look(self, step):
        code = jnp.int32(-1)
        for role, order in self.arrivals.items():
            for k, (owner, h) in enumerate(order):
                dest = self.relays.get((role, owner, h), -1)
                value = owner * 4 + h
                if dest >= 0:
                    there = self.arrivals[dest].index((owner, h))
                    value += 16 * (dest + 1) + 128 * there + 2048 * self.sent[role, dest, owner, h]
                code = jnp.where((self.chip == role) & (step == k), value, code)
        return (code >= 0, (code // 4) % 4, code % 4, (code // 16) % 8 - 1, (code // 128) % 16, code // 2048)

    def service(self, step, serve=None):
        wanted, owner, h, dest, there, k = self.look(step)
        if serve is not None:
            wanted = wanted & serve

        @pl.when(wanted)
        def _():
            here = self.near.at[owner, h]
            gap = self.chip - owner
            self.landed(step, owner, h).wait_recv()

            @pl.when(dest >= 0)
            def _():
                remote(here, here, self.ss.at[k], self.rs.at[there], self.target(dest, self.core)).start()

            @pl.when((gap == 1) | ((gap == 2) & (self.core == 1)))
            def _():
                self.share(owner, h).start()

    def drain(self):
        @pl.when(self.core == 0)
        def _():
            for h in range(HEADS):
                self.share(self.chip, h).wait_send()
        for sender, receiver, owner, heads in self.moves:
            @pl.when(self.chip == sender)
            def _():
                for h in heads:
                    self.move(sender, receiver, owner, h).wait_send()
        for (role, owner, h), receiver in self.relays.items():
            @pl.when(self.chip == role)
            def _():
                self.move(role, receiver, owner, h).wait_send()
        for role, order in self.arrivals.items():
            for owner, h in order:
                if owner == role - 1:
                    @pl.when(self.chip == role)
                    def _():
                        self.share(owner, h).wait_send()
                if owner == role - 2:
                    @pl.when((self.chip == role) & (self.core == 1))
                    def _():
                        self.share(owner, h).wait_send()


def layer_kernel(tokens_hbm, ids, w_in_hbm, w_out_hbm, cot_hbm, output_hbm, grad_tokens_hbm, out_in_hbm, out_out_hbm,
                 out_in, out_out, output, grad_tokens, out_sems, tokens, w_in, w_out, cot, in_sems, normed_t, cot_t, normed, slope, u, kv, qs, gs, att, dq, dk, dv, gated, gh, masks, masks_t,
                 tmp, part, s2, recv1, r2, s3a, s3b, r3a, r3b, t4, r4,
                 kss, krs, ksp, krp, qss, qrs, qsp, qrp, grs, grp,
                 ss1, rs1, sss, rs2, rs3, rs4):
    y, x, z, c = place()
    other = 1 - c
    block = z * 2 + c
    peers = ([device(y, x, z, other)]
             + [device(y, turn(x, d), z, c) for d in (1, 2, 3)]
             + [device(turn(y, d), x, z, c) for d in (1, 2, 3)]
             + [device(y, x, turn(z, d), c) for d in (1, 2, 3)])
    barrier = pltpu.get_barrier_semaphore()
    for t in peers:
        pl.semaphore_signal(barrier, inc=1, device_id=t, device_id_type=MESH)

    tokens_in = pltpu.make_async_copy(tokens_hbm, tokens, in_sems.at[0])
    tokens_in.start()
    w_ins = {}
    for i, col in enumerate((1536, 512, 1024, 0)):
        cols = pl.ds(col, 512)
        w_ins[col] = pltpu.make_async_copy(w_in_hbm.at[:, cols], w_in.at[:, cols], in_sems.at[1 + i])
        w_ins[col].start()
    cot_in = pltpu.make_async_copy(cot_hbm, cot, in_sems.at[5])
    w_out_in = pltpu.make_async_copy(w_out_hbm, w_out, in_sems.at[6])
    cot_in.start()
    w_out_in.start()
    mz, mc = 3 - z, 1 - c

    def mirrored(zz, cc):
        return device(y, x, 3 - zz, 1 - cc)

    before = Gather(kv, (kss, krs, ksp, krp), z, c, lambda zz, cc: device(y, x, zz, cc),
                    OWN_MOVES, RELAYS, ARRIVALS)
    queries = Gather(qs, (qss, qrs, qsp, qrp), mz, mc, mirrored,
                     QUERY_MOVES, QUERY_RELAYS, QUERY_ARRIVALS)
    grads = Gather(gs, (kss, grs, ksp, grp), mz, mc, mirrored,
                   OWN_MOVES, RELAYS, GRAD_ARRIVALS)

    def stats(v):
        center = v - jnp.mean(v, axis=-1, keepdims=True)
        inverse = lax.rsqrt(jnp.mean(center * center, axis=-1, keepdims=True) + EPS)
        return center * inverse, inverse

    def row_loop(size):
        def wrap(body):
            @pl.loop(0, ROWS // size)
            def _(i):
                body(pl.ds(pl.multiple_of(i * size, size), size))
        return wrap

    tokens_in.wait()

    @row_loop(128)
    def _(rows):
        normed[rows, :] = stats(tokens[rows, :].astype(F32))[0].astype(BF16)

    def features(col, width, put):
        @row_loop(256)
        def _(rows):
            half = 0.5 * dot_nn(normed[rows, :], w_in[:, col:col + width])
            t = jnp.tanh(half)
            slope[rows, col:col + width] = 0.5 * (1.0 + t) * (1.0 + half * (1.0 - t))
            put(rows, (half * (1.0 + t)).astype(BF16))

    def put_kv(first, at):
        def put(rows, a):
            for h in range(2):
                kv[0, z, first + h, rows, at:at + 128] = a[:, h * 128:(h + 1) * 128]
        return put

    def put_q(rows, a):
        for h in range(HEADS):
            qs[0, mz, h, rows, :] = a[:, h * 128:(h + 1) * 128]

    def put_u(rows, a):
        u[rows, :] = a

    w_ins[1536].wait()
    features(1536, 256, put_kv(0, 0))
    w_ins[512].wait()
    features(512, 256, put_kv(0, 128))
    pl.semaphore_wait(barrier, len(peers))
    before.start(only=(0, 1))
    features(1792, 256, put_kv(2, 0))
    features(768, 256, put_kv(2, 128))
    before.start(only=(2, 3))
    w_ins[1024].wait()
    features(1024, 512, put_q)
    queries.start(QUERY_MOVES[:4])
    w_ins[0].wait()
    features(0, 512, put_u)

    def ids_of(b):
        b = jnp.clip(b, 0, 7)
        return ids[:, pl.ds(pl.multiple_of(b * ROWS, ROWS), ROWS)].astype(F32)

    own_ids = jnp.transpose(jnp.broadcast_to(ids_of(block), (128, ROWS)))
    own_col = jnp.broadcast_to(own_ids[:, 0:1], (ROWS, ROWS))
    one, nil = jnp.ones((ROWS, ROWS), F32), jnp.zeros((ROWS, ROWS), F32)
    down = lax.broadcasted_iota(jnp.int32, (ROWS, ROWS), 0)
    right = lax.broadcasted_iota(jnp.int32, (ROWS, ROWS), 1)
    for d in range(5):
        same = own_col == jnp.broadcast_to(ids_of(block - d), (ROWS, ROWS))
        same_t = own_col == jnp.broadcast_to(ids_of(block + d), (ROWS, ROWS))
        if d == 0:
            same = same & (right <= down)
            same_t = same_t & (down <= right)
        masks[d] = jnp.where(same, one, nil).astype(BF16)
        masks_t[d] = jnp.where(same_t, one, nil).astype(BF16)

    def pipeline(items, scores, weigh, add):
        ahead = scores(*items[0])
        for i, item in enumerate(items):
            now = ahead
            if i + 1 < len(items):
                ahead = scores(*items[i + 1])
            add(item, weigh(now, item))

    def tiles(where, flip, heads, d):
        out = []
        for h in heads:
            for r in (0, 256):
                cols = (0, 512)
                if isinstance(d, int) and d == 0:
                    cols = ((0, 256), (0, 512))[r // 256] if not flip else ((0, 512), (256, 512))[r // 256]
                out.append(where + (h, d, (r, r + 256), cols))
        return out

    def forward_tiles(items, first=False):
        def scores(e, o, h, d, rows, cols):
            return dot_nt(qs[0, mz, h, rows[0]:rows[1], :], kv[e, o, h, cols[0]:cols[1], 0:128])

        def weigh(now, item):
            e, o, h, d, rows, cols = item
            half = (now * HALF_SCALE).astype(BF16)
            return (half + half * jnp.tanh(half)) * masks[d, rows[0]:rows[1], cols[0]:cols[1]]

        def add(item, w):
            e, o, h, d, rows, cols = item
            a = dot_nn(w, kv[e, o, h, cols[0]:cols[1], 128:256])
            if first:
                att[h, rows[0]:rows[1], :] = a
            else:
                att[h, rows[0]:rows[1], :] += a

        pipeline(items, scores, weigh, add)

    def query_tiles(items, first=False):
        def scores(e, o, h, d, rows, cols):
            keys = slice(cols[0], cols[1])
            mine = slice(rows[0], rows[1])
            return (dot_nt(qs[0, mz, h, mine, :], kv[e, o, h, keys, 0:128]),
                    dot_nt(gs[0, mz, h, mine, :], kv[e, o, h, keys, 128:256]))

        def weigh(now, item):
            e, o, h, d, rows, cols = item
            half = (now[0] * HALF_SCALE).astype(BF16)
            t = jnp.tanh(half)
            a = (t + 1) * masks[d, rows[0]:rows[1], cols[0]:cols[1]]
            return now[1].astype(BF16) * (a + half * a * (1 - t))

        def add(item, ds):
            e, o, h, d, rows, cols = item
            a = dot_nn(ds, kv[e, o, h, cols[0]:cols[1], 0:128])
            if first:
                dq[h, rows[0]:rows[1], :] = a
            else:
                dq[h, rows[0]:rows[1], :] += a

        pipeline(items, scores, weigh, add)

    def key_tiles(items, first=False):
        def scores(e, o, h, d, rows, cols):
            theirs = slice(cols[0], cols[1])
            mine = slice(rows[0], rows[1])
            return (dot_nt(kv[0, z, h, mine, 0:128], qs[e, o, h, theirs, :]),
                    dot_nt(kv[0, z, h, mine, 128:256], gs[e, o, h, theirs, :]))

        def weigh(now, item):
            e, o, h, d, rows, cols = item
            half = (now[0] * HALF_SCALE).astype(BF16)
            t = jnp.tanh(half)
            a = (t + 1) * masks_t[d, rows[0]:rows[1], cols[0]:cols[1]]
            w = half * a
            return w, now[1].astype(BF16) * (a + w * (1 - t))

        def add(item, got):
            e, o, h, d, rows, cols = item
            av = dot_nn(got[0], gs[e, o, h, cols[0]:cols[1], :])
            ak = dot_nn(got[1], qs[e, o, h, cols[0]:cols[1], :])
            if first:
                dv[h, rows[0]:rows[1], :] = av
                dk[h, rows[0]:rows[1], :] = ak
            else:
                dv[h, rows[0]:rows[1], :] += av
                dk[h, rows[0]:rows[1], :] += ak

        pipeline(items, scores, weigh, add)

    def meet(gather, step, compute, flip, also=None):
        there, o, h, _, _, _ = gather.look(step)
        gap = gather.chip - o
        even = 2 * gap
        odd = even + 2 * gather.core - 1

        @pl.when(there & ((gap == 1) | ((gap == 2) & (gather.core == 0))))
        def _():
            gather.share(o, h).wait_recv()
            if also is not None:
                also.share(o, h).wait_recv()
            compute(tiles((0, o), flip, (h,), even) + tiles((1, o), flip, (h,), odd))

        @pl.when(there & (gap == 2) & (gather.core == 1))
        def _():
            compute(tiles((0, o), flip, (h,), even))

    def beside(gather, compute, flip, also=None):
        @pl.when(gather.core == 1)
        def _():
            @pl.loop(0, 2)
            def _(pair):
                heads = (2 * pair, 2 * pair + 1)
                for h in heads:
                    gather.share(gather.chip, h).wait_recv()
                    if also is not None:
                        also.share(gather.chip, h).wait_recv()
                compute(tiles((1, gather.chip), flip, heads, 1))

    def pair_copy(b):
        return remote(s2.at[b], recv1.at[b], ss1.at[b], rs1.at[b], device(y, x, z, other))

    def weight(b, left, cols):
        @pl.loop(0, 4)
        def _(r):
            rows = pl.ds(pl.multiple_of(r * 256, 256), 256)
            tmp[...] = dot_nn(left[rows, :], cols).reshape(16, 2, 8, 512)
            half = pl.ds(pl.multiple_of(r * 128, 128), 128)
            part[b, half, :] = tmp[:, c].reshape(128, 512)
            s2[b, r] = tmp[:, other].reshape(4, 32, 512).astype(BF16)
        pair_copy(b).start()

    def plane_copies(g):
        b = pl.ds(*GROUPS[g])
        out = []
        for d in (1, 2, 3):
            xx, yy = turn(x, d), turn(y, d)
            out.append(remote(s2.at[b, :, xx, :, pl.ds(0, 256)], r2.at[0, d - 1, b], sss.at[g, d - 1],
                              rs2.at[g, d - 1], device(y, xx, z, c)))
            out.append(remote(s2.at[b, yy, :, :, pl.ds(256, 256)], r2.at[1, d - 1, b], sss.at[g, d + 2],
                              rs2.at[g, d + 2], device(yy, x, z, c)))
        return out

    def line_copies(g):
        b = pl.ds(*GROUPS[g])
        out = []
        for d in (1, 2, 3):
            xx, yy = turn(x, d), turn(y, d)
            out.append(remote(s3a.at[b, yy], r3a.at[d - 1, b], sss.at[g, d - 1], rs3.at[g, d - 1],
                              device(yy, x, z, c)))
            out.append(remote(s3b.at[b, xx], r3b.at[d - 1, b], sss.at[g, d + 2], rs3.at[g, d + 2],
                              device(y, xx, z, c)))
        return out

    def chip_copies(g):
        b = pl.ds(*GROUPS[g])
        return [remote(t4.at[turn(z, d), b], r4.at[d - 1, b], sss.at[g, d - 1], rs4.at[g, d - 1],
                       device(y, x, turn(z, d), c)) for d in (1, 2, 3)]

    def blocks_of(g):
        return range(GROUPS[g][0], GROUPS[g][0] + GROUPS[g][1])

    def second(g):
        for b in blocks_of(g):
            pair_copy(b).wait()
            for i in range(4):
                mine = part[b, i * 128:(i + 1) * 128, :].reshape(4, 32, 512)
                s2[b, i] = (mine + recv1[b, i].astype(F32)).astype(BF16)
        for cp in plane_copies(g):
            cp.start()

    def third(g):
        for cp in plane_copies(g):
            cp.wait()
        for b in blocks_of(g):
            a = s2[b, :, x, :, 0:256].astype(F32)
            e = s2[b, y, :, :, 256:512].astype(F32)
            for d in range(3):
                a = a + r2[0, d, b].astype(F32)
                e = e + r2[1, d, b].astype(F32)
            s3a[b] = a.astype(BF16)
            s3b[b] = e.astype(BF16)
        for cp in line_copies(g):
            cp.start()

    def fourth(g):
        for cp in line_copies(g):
            cp.wait()
        for b in blocks_of(g):
            a = s3a[b, y].astype(F32)
            e = s3b[b, x].astype(F32)
            for d in range(3):
                a = a + r3a[d, b].astype(F32)
                e = e + r3b[d, b].astype(F32)
            t4[:, b, :, 0:256] = a.reshape(4, 8, 256)
            t4[:, b, :, 256:512] = e.reshape(4, 8, 256)
        for cp in chip_copies(g):
            cp.start()

    RESULT = {1: 0, 2: 1024, 3: 512, 4: 1536}

    def result_copy(b):
        if b == 0:
            return pltpu.make_async_copy(out_out, out_out_hbm, out_sems.at[2])
        cols = pl.ds(RESULT[b], 512)
        return pltpu.make_async_copy(out_in.at[:, cols], out_in_hbm.at[:, cols], out_sems.at[2 + b])

    def fifth(g):
        for cp in chip_copies(g):
            cp.wait()
        for b in blocks_of(g):
            total = t4[z, b] + r4[0, b] + r4[1, b] + r4[2, b]
            if b == 0:
                out_out[...] = total
            else:
                out_in[:, RESULT[b]:RESULT[b] + 512] = total
            result_copy(b).start()

    forward_tiles(tiles((0, z), False, range(HEADS), 0), first=True)
    cot_in.wait()
    w_out_in.wait()

    @row_loop(128)
    def _(rows):
        normed_t[:, rows] = jnp.transpose(normed[rows, :])
        cot_t[:, rows] = jnp.transpose(cot[rows, :])

    beside(before, forward_tiles, False)
    before.service(0)
    before.service(1)
    for step in range(2):
        queries.arrive(step, roles=(1, 2, 3))

    @pl.loop(0, STEPS)
    def _(step):
        meet(before, step, forward_tiles, False)
        before.service(step + 2)

        @pl.when(step == 3)
        def _():
            queries.start(QUERY_MOVES[4:], share=False)


    @row_loop(256)
    def _(rows):
        a = jnp.concatenate([att[h, rows, :] for h in range(HEADS)], axis=1)
        no, inverse = stats(a)
        uu = u[rows, :].astype(F32)
        g = (no * uu).astype(BF16)
        gated[rows, :] = g
        output[rows, :] = (dot_nn(g, w_out[...]) + tokens[rows, :].astype(F32)).astype(BF16)
        gg = dot_nt(cot[rows, :], w_out[...])
        gh[rows, 0:512] = (gg * no * slope[rows, 0:512]).astype(BF16)
        gn = gg * uu
        back = inverse * (gn - jnp.mean(gn, axis=-1, keepdims=True)
                          - no * jnp.mean(gn * no, axis=-1, keepdims=True))
        back = back.astype(BF16)
        for h in range(HEADS):
            gs[0, mz, h, rows, :] = back[:, h * 128:(h + 1) * 128]

    before.drain()
    grads.start()
    output_out = pltpu.make_async_copy(output, output_hbm, out_sems.at[0])
    output_out.start()
    queries.arrive(0, roles=(0,))
    queries.arrive(1, roles=(0,))
    query_tiles(tiles((0, z), False, range(HEADS), 0), first=True)
    weight(0, cot_t, gated[...])
    weight(1, normed_t, gh[:, 0:512])
    queries.arrive(2, roles=(1,))
    early = mz < 2

    @pl.loop(1, 5)
    def _(d):
        @pl.when(block >= d)
        def _():
            owner = jnp.where(d % 2 == 0, z - d // 2, z - (d + 1) // 2 + c)
            query_tiles(tiles((d % 2, owner), False, range(HEADS), d))

        grads.service(d - 1, serve=early)

        @pl.when(d == 2)
        def _():
            second(0)

    queries.arrive(3, roles=(1,))

    @row_loop(256)
    def _(rows):
        for h in range(HEADS):
            at = 1024 + h * 128
            gh[rows, at:at + 128] = (dq[h, rows, :] * HALF_SCALE * slope[rows, at:at + 128]).astype(BF16)

    weight(2, normed_t, gh[:, 1024:1536])
    key_tiles(tiles((0, mz), True, range(HEADS), 0), first=True)
    beside(grads, key_tiles, True, also=queries)
    second(1)
    third(0)
    late = mz >= 2
    grads.service(0, serve=late)
    for step in range(2, 8):
        queries.arrive(step, roles=(2,))
    for step in range(2, 8):
        queries.arrive(step, roles=(3,))

    @pl.loop(0, STEPS)
    def _(step):
        grads.service(step + 1, serve=late)

        @pl.when(step == 4)
        def _():
            queries.arrive(8, roles=(3,))
            queries.arrive(9, roles=(3,))

        meet(grads, step, key_tiles, True, also=queries)

    @row_loop(256)
    def _(rows):
        for h in range(HEADS):
            at = 512 + h * 128
            gh[rows, at:at + 128] = (dv[h, rows, :] * slope[rows, at:at + 128]).astype(BF16)
            at = 1536 + h * 128
            gh[rows, at:at + 128] = (dk[h, rows, :] * HALF_SCALE * slope[rows, at:at + 128]).astype(BF16)

    weight(3, normed_t, gh[:, 512:1024])
    weight(4, normed_t, gh[:, 1536:2048])
    third(1)
    second(2)

    @row_loop(256)
    def _(rows):
        up = dot_nt(gh[rows, :], w_in[...])
        zhat, inverse = stats(tokens[rows, :].astype(F32))
        back = inverse * (up - jnp.mean(up, axis=-1, keepdims=True)
                          - zhat * jnp.mean(up * zhat, axis=-1, keepdims=True))
        grad_tokens[rows, :] = (back + cot[rows, :].astype(F32)).astype(BF16)

    tokens_out = pltpu.make_async_copy(grad_tokens, grad_tokens_hbm, out_sems.at[1])
    tokens_out.start()
    fourth(0)
    fourth(1)
    third(2)
    fifth(0)
    fifth(1)
    fourth(2)
    queries.drain()
    grads.drain()
    output_out.wait()
    tokens_out.wait()
    fifth(2)
    for b in range(NB):
        result_copy(b).wait()


def finish_kernel(a, b, p, q, out_a, out_b, out_p, out_q, va, vb, vp, vq, ins, outs):
    moves = []
    for i in range(4):
        rows = pl.ds(i * 128, 128)
        moves.append((a.at[rows, :], va.at[rows, :], out_a.at[0, rows, :]))
        moves.append((b.at[rows, :], vb.at[rows, :], out_b.at[0, rows, :]))
    moves.append((p, vp, out_p))
    fetch = [pltpu.make_async_copy(q, vq, ins.at[9])]
    fetch += [pltpu.make_async_copy(src, mid, ins.at[i]) for i, (src, mid, _) in enumerate(moves)]
    store = [pltpu.make_async_copy(mid, dst, outs.at[i]) for i, (_, mid, dst) in enumerate(moves)]
    last = pltpu.make_async_copy(vq, out_q, outs.at[9])
    for cp in fetch:
        cp.start()
    fetch[0].wait()
    last.start()
    for got, put in zip(fetch[1:], store):
        got.wait()
        put.start()
    for put in store:
        put.wait()
    last.wait()


def finish(output, grad_tokens, total_in, total_out):
    hbm = pl.BlockSpec(memory_space=pl.ANY)
    dma = pltpu.SemaphoreType.DMA
    return pl.pallas_call(
        finish_kernel,
        name="finish",
        out_shape=(
            jax.ShapeDtypeStruct((1, ROWS, 1024), BF16),
            jax.ShapeDtypeStruct((1, ROWS, 1024), BF16),
            jax.ShapeDtypeStruct((8, 2048), F32),
            jax.ShapeDtypeStruct((8, 512), F32),
        ),
        in_specs=[hbm] * 4,
        out_specs=(hbm,) * 4,
        scratch_shapes=[
            pltpu.VMEM((ROWS, 1024), BF16),
            pltpu.VMEM((ROWS, 1024), BF16),
            pltpu.VMEM((8, 2048), F32),
            pltpu.VMEM((8, 512), F32),
            dma((10,)), dma((10,)),
        ],
    )(output, grad_tokens, total_in, total_out)


def local(tokens_in, user_ids, w_in, w_out, cotangent):
    vmem = pl.BlockSpec(memory_space=pltpu.VMEM)
    hbm = pl.BlockSpec(memory_space=pl.ANY)
    dma = pltpu.SemaphoreType.DMA

    output, grad_tokens, total_in, total_out = pl.pallas_call(
        layer_kernel,
        name="layer",
        out_shape=(
            jax.ShapeDtypeStruct((ROWS, 1024), BF16),
            jax.ShapeDtypeStruct((ROWS, 1024), BF16),
            jax.ShapeDtypeStruct((8, 2048), F32),
            jax.ShapeDtypeStruct((8, 512), F32),
        ),
        in_specs=[hbm, vmem, hbm, hbm, hbm],
        out_specs=(hbm,) * 4,
        scratch_shapes=[
            pltpu.VMEM((8, 2048), F32),
            pltpu.VMEM((8, 512), F32),
            pltpu.VMEM((ROWS, 1024), BF16),
            pltpu.VMEM((ROWS, 1024), BF16),
            dma((7,)),
            pltpu.VMEM((ROWS, 1024), BF16),
            pltpu.VMEM((1024, 2048), BF16),
            pltpu.VMEM((512, 1024), BF16),
            pltpu.VMEM((ROWS, 1024), BF16),
            dma((7,)),
            pltpu.VMEM((1024, ROWS), BF16),
            pltpu.VMEM((1024, ROWS), BF16),
            pltpu.VMEM((ROWS, 1024), BF16),
            pltpu.VMEM((ROWS, 2048), F32),
            pltpu.VMEM((ROWS, 512), BF16),
            pltpu.VMEM((2, 4, 4, ROWS, 256), BF16),
            pltpu.VMEM((2, 4, 4, ROWS, 128), BF16),
            pltpu.VMEM((2, 4, 4, ROWS, 128), BF16),
            pltpu.VMEM((4, ROWS, 128), F32),
            pltpu.VMEM((4, ROWS, 128), F32),
            pltpu.VMEM((4, ROWS, 128), F32),
            pltpu.VMEM((4, ROWS, 128), F32),
            pltpu.VMEM((ROWS, 512), BF16),
            pltpu.VMEM((ROWS, 2048), BF16),
            pltpu.VMEM((5, ROWS, ROWS), BF16),
            pltpu.VMEM((5, ROWS, ROWS), BF16),
            pltpu.VMEM((16, 2, 8, 512), F32),
            pltpu.VMEM((NB, 512, 512), F32),
            pltpu.VMEM((NB, 4, 4, 32, 512), BF16),
            pltpu.VMEM((NB, 4, 4, 32, 512), BF16),
            pltpu.VMEM((2, 3, NB, 4, 32, 256), BF16),
            pltpu.VMEM((NB, 4, 32, 256), BF16),
            pltpu.VMEM((NB, 4, 32, 256), BF16),
            pltpu.VMEM((3, NB, 32, 256), BF16),
            pltpu.VMEM((3, NB, 32, 256), BF16),
            pltpu.VMEM((4, NB, 8, 512), F32),
            pltpu.VMEM((3, NB, 8, 512), F32),
            dma((9,)), dma((10,)), dma((8,)), dma((8,)),
            dma((8,)), dma((10,)), dma((8,)), dma((8,)),
            dma((10,)), dma((8,)),
            dma((NB,)), dma((NB,)), dma((3, 6)), dma((3, 6)), dma((3, 6)), dma((3, 3)),
        ],
        compiler_params=pltpu.CompilerParams(
            collective_id=0, has_side_effects=True, vmem_limit_bytes=67043328),
    )(tokens_in[0], user_ids, w_in, w_out, cotangent[0])
    output, grad_tokens, total_in, total_out = finish(output, grad_tokens, total_in, total_out)
    return output, grad_tokens, total_in, total_out.T


def solution(mesh):
    in_specs = (P("dp", "seq", None), P("dp", None), P(), P(), P("dp", "seq", None))
    out_specs = (
        P("dp", "seq", None),
        P("dp", "seq", None),
        P(("dp", "seq"), None),
        P(None, ("dp", "seq")),
    )
    return jax.shard_map(local, mesh=mesh, in_specs=in_specs, out_specs=out_specs, check_vma=False)
```

```python
import math

import jax
import jax.numpy as jnp
from jax import lax
from jax.experimental import pallas as pl
from jax.experimental.pallas import tpu as pltpu
from jax.sharding import PartitionSpec as P

HEADS = 4
HD = 128
ROWS = 512
F32 = jnp.float32
BF16 = jnp.bfloat16
EPS = 1e-05
HALF_SCALE = 0.5 / math.sqrt(HD)
MESH = pl.DeviceIdType.MESH
NB = 5
GROUPS = ((0, 2), (2, 1), (3, 2))

OWN_MOVES = (
    (0, 1, 0, (0, 1, 2, 3)),
    (0, 3, 0, (0, 1)),
    (1, 2, 1, (1, 2, 3)),
    (1, 0, 1, (0, 1, 2)),
    (2, 3, 2, (0, 1, 2, 3)),
)
RELAYS = {
    (1, 0, 2): 2, (1, 0, 3): 2,
    (0, 1, 0): 3, (0, 1, 1): 3, (0, 1, 2): 3,
    (3, 0, 0): 2, (3, 0, 1): 2, (3, 1, 0): 2,
    (2, 1, 3): 3,
}
ARRIVALS = {
    0: ((1, 0), (1, 1), (1, 2)),
    1: ((0, 0), (0, 1), (0, 2), (0, 3)),
    2: ((1, 1), (0, 0), (1, 2), (0, 1), (1, 3), (1, 0), (0, 2), (0, 3)),
    3: ((2, 0), (0, 0), (2, 1), (0, 1), (2, 2), (1, 0), (2, 3), (1, 1), (1, 2), (1, 3)),
}
STEPS = 10
QUERY_MOVES = (
    (0, 1, 0, (0, 1)),
    (0, 3, 0, (2, 3)),
    (1, 2, 1, (0, 1, 2, 3)),
    (2, 3, 2, (0, 1, 2, 3)),
    (1, 0, 1, (3, 2)),
    (0, 1, 0, (2, 3)),
)
QUERY_RELAYS = {
    (1, 0, 0): 2, (1, 0, 1): 2,
    (3, 0, 2): 2, (3, 0, 3): 2,
    (2, 1, 0): 3, (2, 1, 1): 3,
    (0, 1, 3): 3, (0, 1, 2): 3,
}
QUERY_ARRIVALS = {
    0: ((1, 3), (1, 2)),
    1: ((0, 0), (0, 1), (0, 2), (0, 3)),
    2: ((1, 0), (1, 1), (1, 2), (1, 3), (0, 2), (0, 3), (0, 0), (0, 1)),
    3: ((0, 2), (0, 3), (2, 0), (2, 1), (2, 2), (2, 3), (1, 0), (1, 1), (1, 3), (1, 2)),
}
GRAD_ARRIVALS = {
    0: ((1, 0), (1, 1), (1, 2)),
    1: ((0, 0), (0, 1), (0, 2), (0, 3)),
    2: ((1, 1), (1, 2), (0, 0), (1, 3), (0, 2), (0, 1), (0, 3), (1, 0)),
    3: ((2, 0), (2, 1), (0, 0), (2, 2), (0, 1), (2, 3), (1, 0), (1, 1), (1, 3), (1, 2)),
}


def place():
    dp, seq = lax.axis_index("dp"), lax.axis_index("seq")
    return dp // 4, dp % 4, seq // 2, seq % 2


def device(y, x, z, core):
    return {"dp": y * 4 + x, "seq": z * 2 + core}


def turn(i, d):
    return lax.rem(i + d, 4)


def remote(src, dst, send, recv, target):
    return pltpu.make_async_remote_copy(
        src_ref=src, dst_ref=dst, send_sem=send, recv_sem=recv,
        device_id=target, device_id_type=MESH)


def dot_nn(a, b):
    return jnp.dot(a, b, preferred_element_type=F32)


def dot_nt(a, b):
    return lax.dot_general(a, b, (((1,), (1,)), ((), ())), preferred_element_type=F32)


def dot_tn(a, b):
    return lax.dot_general(a, b, (((0,), (0,)), ((), ())), preferred_element_type=F32)


class Gather:
    def __init__(self, buf, sems, chip, core, target, moves, relays, arrivals):
        self.buf, self.near, self.far = buf, buf.at[0], buf.at[1]
        self.ss, self.rs, self.sp, self.rp = sems
        self.chip, self.core, self.target = chip, core, target
        self.moves, self.relays, self.arrivals = moves, relays, arrivals
        self.sent = {}
        for role in range(4):
            mine = [(receiver, owner, h) for sender, receiver, owner, heads in moves if sender == role for h in heads]
            mine += [(receiver, owner, h) for (sender, owner, h), receiver in relays.items() if sender == role]
            for k, (receiver, owner, h) in enumerate(mine):
                self.sent[role, receiver, owner, h] = k

    def move(self, sender, receiver, owner, h):
        return remote(self.near.at[owner, h], self.near.at[owner, h], self.ss.at[self.sent[sender, receiver, owner, h]],
                      self.rs.at[self.arrivals[receiver].index((owner, h))], self.target(receiver, self.core))

    def landed(self, step, owner, h):
        here = self.near.at[owner, h]
        return remote(here, here, self.ss.at[0], self.rs.at[step], self.target(turn(self.chip, 1), self.core))

    def share(self, owner, h):
        k = jnp.where(self.chip - owner == 1, 4, 0) + h
        return remote(self.near.at[owner, h], self.far.at[owner, h], self.sp.at[k],
                      self.rp.at[k], self.target(self.chip, 1 - self.core))

    def start(self, moves=None, share=True, only=(0, 1, 2, 3)):
        if share:
            @pl.when(self.core == 0)
            def _():
                for h in only:
                    self.share(self.chip, h).start()
        for sender, receiver, owner, heads in (self.moves if moves is None else moves):
            @pl.when(self.chip == sender)
            def _():
                for h in heads:
                    if h in only:
                        self.move(sender, receiver, owner, h).start()

    def arrive(self, step, roles=(0, 1, 2, 3)):
        for role in roles:
            order = self.arrivals.get(role, ())
            if step >= len(order):
                continue
            owner, h = order[step]

            @pl.when(self.chip == role)
            def _():
                self.landed(step, owner, h).wait_recv()
                if (role, owner, h) in self.relays:
                    self.move(role, self.relays[role, owner, h], owner, h).start()
                if owner == role - 1:
                    self.share(owner, h).start()
                if owner == role - 2:
                    @pl.when(self.core == 1)
                    def _():
                        self.share(owner, h).start()

    def look(self, step):
        code = jnp.int32(-1)
        for role, order in self.arrivals.items():
            for k, (owner, h) in enumerate(order):
                dest = self.relays.get((role, owner, h), -1)
                value = owner * 4 + h
                if dest >= 0:
                    there = self.arrivals[dest].index((owner, h))
                    value += 16 * (dest + 1) + 128 * there + 2048 * self.sent[role, dest, owner, h]
                code = jnp.where((self.chip == role) & (step == k), value, code)
        return (code >= 0, (code // 4) % 4, code % 4, (code // 16) % 8 - 1, (code // 128) % 16, code // 2048)

    def service(self, step, serve=None):
        wanted, owner, h, dest, there, k = self.look(step)
        if serve is not None:
            wanted = wanted & serve

        @pl.when(wanted)
        def _():
            here = self.near.at[owner, h]
            gap = self.chip - owner
            self.landed(step, owner, h).wait_recv()

            @pl.when(dest >= 0)
            def _():
                remote(here, here, self.ss.at[k], self.rs.at[there], self.target(dest, self.core)).start()

            @pl.when((gap == 1) | ((gap == 2) & (self.core == 1)))
            def _():
                self.share(owner, h).start()

    def drain(self):
        @pl.when(self.core == 0)
        def _():
            for h in range(HEADS):
                self.share(self.chip, h).wait_send()
        for sender, receiver, owner, heads in self.moves:
            @pl.when(self.chip == sender)
            def _():
                for h in heads:
                    self.move(sender, receiver, owner, h).wait_send()
        for (role, owner, h), receiver in self.relays.items():
            @pl.when(self.chip == role)
            def _():
                self.move(role, receiver, owner, h).wait_send()
        for role, order in self.arrivals.items():
            for owner, h in order:
                if owner == role - 1:
                    @pl.when(self.chip == role)
                    def _():
                        self.share(owner, h).wait_send()
                if owner == role - 2:
                    @pl.when((self.chip == role) & (self.core == 1))
                    def _():
                        self.share(owner, h).wait_send()


def layer_kernel(tokens_hbm, ids, w_in_hbm, w_out_hbm, cot_hbm, output_hbm, grad_tokens_hbm, out_in_hbm, out_out_hbm,
                 out_in, out_out, output, grad_tokens, out_sems, tokens, w_in, w_out, cot, in_sems, normed_t, cot_t, normed, slope, u, kv, qs, gs, att, dq, dk, dv, gated, gh, masks, masks_t,
                 part, s2, recv1, r2, s3a, s3b, r3a, r3b, t4, r4,
                 kss, krs, ksp, krp, qss, qrs, qsp, qrp, grs, grp,
                 ss1, rs1, sss, rs2, rs3, rs4):
    y, x, z, c = place()
    other = 1 - c
    block = z * 2 + c
    peers = ([device(y, x, z, other)]
             + [device(y, turn(x, d), z, c) for d in (1, 2, 3)]
             + [device(turn(y, d), x, z, c) for d in (1, 2, 3)]
             + [device(y, x, turn(z, d), c) for d in (1, 2, 3)])
    barrier = pltpu.get_barrier_semaphore()
    for t in peers:
        pl.semaphore_signal(barrier, inc=1, device_id=t, device_id_type=MESH)

    tokens_in = pltpu.make_async_copy(tokens_hbm, tokens, in_sems.at[0])
    tokens_in.start()
    w_ins = {}
    for i, col in enumerate((1536, 512, 1024, 0)):
        cols = pl.ds(col, 512)
        w_ins[col] = pltpu.make_async_copy(w_in_hbm.at[:, cols], w_in.at[:, cols], in_sems.at[1 + i])
        w_ins[col].start()
    cot_in = pltpu.make_async_copy(cot_hbm, cot, in_sems.at[5])
    w_out_in = pltpu.make_async_copy(w_out_hbm, w_out, in_sems.at[6])
    cot_in.start()
    w_out_in.start()
    mz, mc = 3 - z, 1 - c

    def mirrored(zz, cc):
        return device(y, x, 3 - zz, 1 - cc)

    before = Gather(kv, (kss, krs, ksp, krp), z, c, lambda zz, cc: device(y, x, zz, cc),
                    OWN_MOVES, RELAYS, ARRIVALS)
    queries = Gather(qs, (qss, qrs, qsp, qrp), mz, mc, mirrored,
                     QUERY_MOVES, QUERY_RELAYS, QUERY_ARRIVALS)
    grads = Gather(gs, (kss, grs, ksp, grp), mz, mc, mirrored,
                   OWN_MOVES, RELAYS, GRAD_ARRIVALS)

    def stats(v):
        center = v - jnp.mean(v, axis=-1, keepdims=True)
        inverse = lax.rsqrt(jnp.mean(center * center, axis=-1, keepdims=True) + EPS)
        return center * inverse, inverse

    def row_loop(size):
        def wrap(body):
            @pl.loop(0, ROWS // size)
            def _(i):
                body(pl.ds(pl.multiple_of(i * size, size), size))
        return wrap

    tokens_in.wait()

    @row_loop(128)
    def _(rows):
        normed[rows, :] = stats(tokens[rows, :].astype(F32))[0].astype(BF16)

    def features(col, width, put):
        @row_loop(256)
        def _(rows):
            half = 0.5 * dot_nn(normed[rows, :], w_in[:, col:col + width])
            t = jnp.tanh(half)
            slope[rows, col:col + width] = 0.5 * (1.0 + t) * (1.0 + half * (1.0 - t))
            put(rows, (half * (1.0 + t)).astype(BF16))

    def put_kv(first, at):
        def put(rows, a):
            for h in range(2):
                kv[0, z, first + h, rows, at:at + 128] = a[:, h * 128:(h + 1) * 128]
        return put

    def put_q(rows, a):
        for h in range(HEADS):
            qs[0, mz, h, rows, :] = a[:, h * 128:(h + 1) * 128]

    def put_u(rows, a):
        u[rows, :] = a

    w_ins[1536].wait()
    features(1536, 256, put_kv(0, 0))
    w_ins[512].wait()
    features(512, 256, put_kv(0, 128))
    pl.semaphore_wait(barrier, len(peers))
    before.start(only=(0, 1))
    features(1792, 256, put_kv(2, 0))
    features(768, 256, put_kv(2, 128))
    before.start(only=(2, 3))
    w_ins[1024].wait()
    features(1024, 512, put_q)
    queries.start(QUERY_MOVES[:4])
    w_ins[0].wait()
    features(0, 512, put_u)

    def ids_of(b):
        b = jnp.clip(b, 0, 7)
        return ids[:, pl.ds(pl.multiple_of(b * ROWS, ROWS), ROWS)].astype(F32)

    own_ids = jnp.transpose(jnp.broadcast_to(ids_of(block), (128, ROWS)))
    own_col = jnp.broadcast_to(own_ids[:, 0:1], (ROWS, ROWS))
    one, nil = jnp.ones((ROWS, ROWS), F32), jnp.zeros((ROWS, ROWS), F32)
    down = lax.broadcasted_iota(jnp.int32, (ROWS, ROWS), 0)
    right = lax.broadcasted_iota(jnp.int32, (ROWS, ROWS), 1)
    for d in range(5):
        same = own_col == jnp.broadcast_to(ids_of(block - d), (ROWS, ROWS))
        same_t = own_col == jnp.broadcast_to(ids_of(block + d), (ROWS, ROWS))
        if d == 0:
            same = same & (right <= down)
            same_t = same_t & (down <= right)
        masks[d] = jnp.where(same, one, nil).astype(BF16)
        masks_t[d] = jnp.where(same_t, one, nil).astype(BF16)

    def pipeline(items, scores, weigh, add):
        ahead = scores(*items[0])
        for i, item in enumerate(items):
            now = ahead
            if i + 1 < len(items):
                ahead = scores(*items[i + 1])
            add(item, weigh(now, item))

    def tiles(where, flip, heads, d):
        out = []
        for h in heads:
            for r in (0, 256):
                cols = (0, 512)
                if isinstance(d, int) and d == 0:
                    cols = ((0, 256), (0, 512))[r // 256] if not flip else ((0, 512), (256, 512))[r // 256]
                out.append(where + (h, d, (r, r + 256), cols))
        return out

    def forward_tiles(items, first=False):
        def scores(e, o, h, d, rows, cols):
            return dot_nt(qs[0, mz, h, rows[0]:rows[1], :], kv[e, o, h, cols[0]:cols[1], 0:128])

        def weigh(now, item):
            e, o, h, d, rows, cols = item
            half = (now * HALF_SCALE).astype(BF16)
            return (half + half * jnp.tanh(half)) * masks[d, rows[0]:rows[1], cols[0]:cols[1]]

        def add(item, w):
            e, o, h, d, rows, cols = item
            a = dot_nn(w, kv[e, o, h, cols[0]:cols[1], 128:256])
            if first:
                att[h, rows[0]:rows[1], :] = a
            else:
                att[h, rows[0]:rows[1], :] += a

        pipeline(items, scores, weigh, add)

    def query_tiles(items, first=False):
        def scores(e, o, h, d, rows, cols):
            keys = slice(cols[0], cols[1])
            mine = slice(rows[0], rows[1])
            return (dot_nt(qs[0, mz, h, mine, :], kv[e, o, h, keys, 0:128]),
                    dot_nt(gs[0, mz, h, mine, :], kv[e, o, h, keys, 128:256]))

        def weigh(now, item):
            e, o, h, d, rows, cols = item
            half = (now[0] * HALF_SCALE).astype(BF16)
            t = jnp.tanh(half)
            a = (t + 1) * masks[d, rows[0]:rows[1], cols[0]:cols[1]]
            return now[1].astype(BF16) * (a + half * a * (1 - t))

        def add(item, ds):
            e, o, h, d, rows, cols = item
            a = dot_nn(ds, kv[e, o, h, cols[0]:cols[1], 0:128])
            if first:
                dq[h, rows[0]:rows[1], :] = a
            else:
                dq[h, rows[0]:rows[1], :] += a

        pipeline(items, scores, weigh, add)

    def key_tiles(items, first=False):
        def scores(e, o, h, d, rows, cols):
            theirs = slice(cols[0], cols[1])
            mine = slice(rows[0], rows[1])
            return (dot_nt(kv[0, z, h, mine, 0:128], qs[e, o, h, theirs, :]),
                    dot_nt(kv[0, z, h, mine, 128:256], gs[e, o, h, theirs, :]))

        def weigh(now, item):
            e, o, h, d, rows, cols = item
            half = (now[0] * HALF_SCALE).astype(BF16)
            t = jnp.tanh(half)
            a = (t + 1) * masks_t[d, rows[0]:rows[1], cols[0]:cols[1]]
            w = half * a
            return w, now[1].astype(BF16) * (a + w * (1 - t))

        def add(item, got):
            e, o, h, d, rows, cols = item
            av = dot_nn(got[0], gs[e, o, h, cols[0]:cols[1], :])
            ak = dot_nn(got[1], qs[e, o, h, cols[0]:cols[1], :])
            if first:
                dv[h, rows[0]:rows[1], :] = av
                dk[h, rows[0]:rows[1], :] = ak
            else:
                dv[h, rows[0]:rows[1], :] += av
                dk[h, rows[0]:rows[1], :] += ak

        pipeline(items, scores, weigh, add)

    def meet(gather, step, compute, flip, also=None):
        there, o, h, _, _, _ = gather.look(step)
        gap = gather.chip - o
        even = 2 * gap
        odd = even + 2 * gather.core - 1

        @pl.when(there & ((gap == 1) | ((gap == 2) & (gather.core == 0))))
        def _():
            gather.share(o, h).wait_recv()
            if also is not None:
                also.share(o, h).wait_recv()
            compute(tiles((0, o), flip, (h,), even) + tiles((1, o), flip, (h,), odd))

        @pl.when(there & (gap == 2) & (gather.core == 1))
        def _():
            compute(tiles((0, o), flip, (h,), even))

    def beside(gather, compute, flip, also=None):
        @pl.when(gather.core == 1)
        def _():
            @pl.loop(0, 2)
            def _(pair):
                heads = (2 * pair, 2 * pair + 1)
                for h in heads:
                    gather.share(gather.chip, h).wait_recv()
                    if also is not None:
                        also.share(gather.chip, h).wait_recv()
                compute(tiles((1, gather.chip), flip, heads, 1))

    def pair_copy(b):
        return remote(s2.at[b], recv1.at[b], ss1.at[b], rs1.at[b], device(y, x, z, other))

    def weight(b, left, cols):
        ahead = dot_nn(left[0:256, :], cols)
        for r in range(4):
            now = ahead.reshape(16, 2, 8, 512)
            if r < 3:
                ahead = dot_nn(left[(r + 1) * 256:(r + 2) * 256, :], cols)
            even, odd = now[:, 0].reshape(128, 512), now[:, 1].reshape(128, 512)
            part[b, r * 128:(r + 1) * 128, :] = jnp.where(c == 0, even, odd)
            s2[b, r] = jnp.where(c == 0, odd, even).reshape(4, 32, 512).astype(BF16)
        pair_copy(b).start()

    def plane_copies(g):
        b = pl.ds(*GROUPS[g])
        out = []
        for d in (1, 2, 3):
            xx, yy = turn(x, d), turn(y, d)
            out.append(remote(s2.at[b, :, xx, :, pl.ds(0, 256)], r2.at[0, d - 1, b], sss.at[g, d - 1],
                              rs2.at[g, d - 1], device(y, xx, z, c)))
            out.append(remote(s2.at[b, yy, :, :, pl.ds(256, 256)], r2.at[1, d - 1, b], sss.at[g, d + 2],
                              rs2.at[g, d + 2], device(yy, x, z, c)))
        return out

    def line_copies(g):
        b = pl.ds(*GROUPS[g])
        out = []
        for d in (1, 2, 3):
            xx, yy = turn(x, d), turn(y, d)
            out.append(remote(s3a.at[b, yy], r3a.at[d - 1, b], sss.at[g, d - 1], rs3.at[g, d - 1],
                              device(yy, x, z, c)))
            out.append(remote(s3b.at[b, xx], r3b.at[d - 1, b], sss.at[g, d + 2], rs3.at[g, d + 2],
                              device(y, xx, z, c)))
        return out

    def chip_copies(g):
        b = pl.ds(*GROUPS[g])
        return [remote(t4.at[turn(z, d), b], r4.at[d - 1, b], sss.at[g, d - 1], rs4.at[g, d - 1],
                       device(y, x, turn(z, d), c)) for d in (1, 2, 3)]

    def blocks_of(g):
        return range(GROUPS[g][0], GROUPS[g][0] + GROUPS[g][1])

    def second(g):
        for b in blocks_of(g):
            pair_copy(b).wait()
            for i in range(4):
                mine = part[b, i * 128:(i + 1) * 128, :].reshape(4, 32, 512)
                s2[b, i] = (mine + recv1[b, i].astype(F32)).astype(BF16)
        for cp in plane_copies(g):
            cp.start()

    def third(g):
        for cp in plane_copies(g):
            cp.wait()
        for b in blocks_of(g):
            a = s2[b, :, x, :, 0:256].astype(F32)
            e = s2[b, y, :, :, 256:512].astype(F32)
            for d in range(3):
                a = a + r2[0, d, b].astype(F32)
                e = e + r2[1, d, b].astype(F32)
            s3a[b] = a.astype(BF16)
            s3b[b] = e.astype(BF16)
        for cp in line_copies(g):
            cp.start()

    def fourth(g):
        for cp in line_copies(g):
            cp.wait()
        for b in blocks_of(g):
            a = s3a[b, y].astype(F32)
            e = s3b[b, x].astype(F32)
            for d in range(3):
                a = a + r3a[d, b].astype(F32)
                e = e + r3b[d, b].astype(F32)
            t4[:, b, :, 0:256] = a.reshape(4, 8, 256)
            t4[:, b, :, 256:512] = e.reshape(4, 8, 256)
        for cp in chip_copies(g):
            cp.start()

    RESULT = {1: 0, 2: 1024, 3: 512, 4: 1536}

    def result_copy(b):
        if b == 0:
            return pltpu.make_async_copy(out_out, out_out_hbm, out_sems.at[2])
        cols = pl.ds(RESULT[b], 512)
        return pltpu.make_async_copy(out_in.at[:, cols], out_in_hbm.at[:, cols], out_sems.at[2 + b])

    def fifth(g):
        for cp in chip_copies(g):
            cp.wait()
        for b in blocks_of(g):
            total = t4[z, b] + r4[0, b] + r4[1, b] + r4[2, b]
            if b == 0:
                out_out[...] = total
            else:
                out_in[:, RESULT[b]:RESULT[b] + 512] = total
            result_copy(b).start()

    forward_tiles(tiles((0, z), False, range(HEADS), 0), first=True)
    cot_in.wait()
    w_out_in.wait()

    @row_loop(128)
    def _(rows):
        normed_t[:, rows] = jnp.transpose(normed[rows, :])
        cot_t[:, rows] = jnp.transpose(cot[rows, :])

    beside(before, forward_tiles, False)
    before.service(0)
    before.service(1)
    for step in range(2):
        queries.arrive(step, roles=(1, 2, 3))

    @pl.loop(0, STEPS)
    def _(step):
        meet(before, step, forward_tiles, False)
        before.service(step + 2)

        @pl.when(step == 3)
        def _():
            queries.start(QUERY_MOVES[4:], share=False)


    @row_loop(256)
    def _(rows):
        a = jnp.concatenate([att[h, rows, :] for h in range(HEADS)], axis=1)
        no, inverse = stats(a)
        uu = u[rows, :].astype(F32)
        g = (no * uu).astype(BF16)
        gated[rows, :] = g
        gg = dot_nt(cot[rows, :], w_out[...])
        gh[rows, 0:512] = (gg * no * slope[rows, 0:512]).astype(BF16)
        gn = gg * uu
        back = inverse * (gn - jnp.mean(gn, axis=-1, keepdims=True)
                          - no * jnp.mean(gn * no, axis=-1, keepdims=True))
        back = back.astype(BF16)
        for h in range(HEADS):
            gs[0, mz, h, rows, :] = back[:, h * 128:(h + 1) * 128]

    pl.when(mz < 3)(before.drain)
    grads.start()
    queries.arrive(0, roles=(0,))
    queries.arrive(1, roles=(0,))
    query_tiles(tiles((0, z), False, range(HEADS), 0), first=True)
    weight(0, cot_t, gated[...])
    weight(1, normed_t, gh[:, 0:512])
    queries.arrive(2, roles=(1,))
    early = mz < 2

    @pl.loop(1, 5)
    def _(d):
        @pl.when(block >= d)
        def _():
            owner = jnp.where(d % 2 == 0, z - d // 2, z - (d + 1) // 2 + c)
            query_tiles(tiles((d % 2, owner), False, range(HEADS), d))

        grads.service(d - 1, serve=early)

        @pl.when(d == 2)
        def _():
            second(0)

    queries.arrive(3, roles=(1,))

    @row_loop(256)
    def _(rows):
        for h in range(HEADS):
            at = 1024 + h * 128
            gh[rows, at:at + 128] = (dq[h, rows, :] * HALF_SCALE * slope[rows, at:at + 128]).astype(BF16)

    weight(2, normed_t, gh[:, 1024:1536])
    key_tiles(tiles((0, mz), True, range(HEADS), 0), first=True)
    beside(grads, key_tiles, True, also=queries)
    second(1)
    late = mz >= 2
    pl.when(mz == 3)(before.drain)
    grads.service(0, serve=late)
    for step in range(2, 8):
        queries.arrive(step, roles=(2,))
    for step in range(2, 8):
        queries.arrive(step, roles=(3,))

    @pl.loop(0, STEPS)
    def _(step):
        grads.service(step + 1, serve=late)

        @pl.when(step == 3)
        def _():
            third(0)

        @pl.when(step == 4)
        def _():
            queries.arrive(8, roles=(3,))
            queries.arrive(9, roles=(3,))

        meet(grads, step, key_tiles, True, also=queries)

    @row_loop(256)
    def _(rows):
        for h in range(HEADS):
            at = 512 + h * 128
            gh[rows, at:at + 128] = (dv[h, rows, :] * slope[rows, at:at + 128]).astype(BF16)
            at = 1536 + h * 128
            gh[rows, at:at + 128] = (dk[h, rows, :] * HALF_SCALE * slope[rows, at:at + 128]).astype(BF16)

    weight(3, normed_t, gh[:, 512:1024])
    weight(4, normed_t, gh[:, 1536:2048])
    third(1)
    second(2)

    @row_loop(256)
    def _(rows):
        up = dot_nt(gh[rows, :], w_in[...])
        zhat, inverse = stats(tokens[rows, :].astype(F32))
        back = inverse * (up - jnp.mean(up, axis=-1, keepdims=True)
                          - zhat * jnp.mean(up * zhat, axis=-1, keepdims=True))
        grad_tokens[rows, :] = (back + cot[rows, :].astype(F32)).astype(BF16)

    tokens_out = pltpu.make_async_copy(grad_tokens, grad_tokens_hbm, out_sems.at[1])
    tokens_out.start()
    fourth(0)
    fourth(1)

    @row_loop(256)
    def _(rows):
        output[rows, :] = (dot_nn(gated[rows, :], w_out[...]) + tokens[rows, :].astype(F32)).astype(BF16)

    output_out = pltpu.make_async_copy(output, output_hbm, out_sems.at[0])
    output_out.start()
    third(2)
    fifth(0)
    fifth(1)
    fourth(2)
    queries.drain()
    grads.drain()
    output_out.wait()
    tokens_out.wait()
    fifth(2)
    for b in range(NB):
        result_copy(b).wait()


def finish_kernel(a, b, p, q, out_a, out_b, out_p, out_q, va, vb, vp, vq, ins, outs):
    moves = []
    for i in range(4):
        rows = pl.ds(i * 128, 128)
        moves.append((a.at[rows, :], va.at[rows, :], out_a.at[0, rows, :]))
        moves.append((b.at[rows, :], vb.at[rows, :], out_b.at[0, rows, :]))
    moves.append((p, vp, out_p))
    fetch = [pltpu.make_async_copy(q, vq, ins.at[9])]
    fetch += [pltpu.make_async_copy(src, mid, ins.at[i]) for i, (src, mid, _) in enumerate(moves)]
    store = [pltpu.make_async_copy(mid, dst, outs.at[i]) for i, (_, mid, dst) in enumerate(moves)]
    last = pltpu.make_async_copy(vq, out_q, outs.at[9])
    for cp in fetch:
        cp.start()
    fetch[0].wait()
    last.start()
    for got, put in zip(fetch[1:], store):
        got.wait()
        put.start()
    for put in store:
        put.wait()
    last.wait()


def finish(output, grad_tokens, total_in, total_out):
    hbm = pl.BlockSpec(memory_space=pl.ANY)
    dma = pltpu.SemaphoreType.DMA
    return pl.pallas_call(
        finish_kernel,
        name="finish",
        out_shape=(
            jax.ShapeDtypeStruct((1, ROWS, 1024), BF16),
            jax.ShapeDtypeStruct((1, ROWS, 1024), BF16),
            jax.ShapeDtypeStruct((8, 2048), F32),
            jax.ShapeDtypeStruct((8, 512), F32),
        ),
        in_specs=[hbm] * 4,
        out_specs=(hbm,) * 4,
        scratch_shapes=[
            pltpu.VMEM((ROWS, 1024), BF16),
            pltpu.VMEM((ROWS, 1024), BF16),
            pltpu.VMEM((8, 2048), F32),
            pltpu.VMEM((8, 512), F32),
            dma((10,)), dma((10,)),
        ],
    )(output, grad_tokens, total_in, total_out)


def local(tokens_in, user_ids, w_in, w_out, cotangent):
    vmem = pl.BlockSpec(memory_space=pltpu.VMEM)
    hbm = pl.BlockSpec(memory_space=pl.ANY)
    dma = pltpu.SemaphoreType.DMA

    output, grad_tokens, total_in, total_out = pl.pallas_call(
        layer_kernel,
        name="layer",
        out_shape=(
            jax.ShapeDtypeStruct((ROWS, 1024), BF16),
            jax.ShapeDtypeStruct((ROWS, 1024), BF16),
            jax.ShapeDtypeStruct((8, 2048), F32),
            jax.ShapeDtypeStruct((8, 512), F32),
        ),
        in_specs=[hbm, vmem, hbm, hbm, hbm],
        out_specs=(hbm,) * 4,
        scratch_shapes=[
            pltpu.VMEM((8, 2048), F32),
            pltpu.VMEM((8, 512), F32),
            pltpu.VMEM((ROWS, 1024), BF16),
            pltpu.VMEM((ROWS, 1024), BF16),
            dma((7,)),
            pltpu.VMEM((ROWS, 1024), BF16),
            pltpu.VMEM((1024, 2048), BF16),
            pltpu.VMEM((512, 1024), BF16),
            pltpu.VMEM((ROWS, 1024), BF16),
            dma((7,)),
            pltpu.VMEM((1024, ROWS), BF16),
            pltpu.VMEM((1024, ROWS), BF16),
            pltpu.VMEM((ROWS, 1024), BF16),
            pltpu.VMEM((ROWS, 2048), F32),
            pltpu.VMEM((ROWS, 512), BF16),
            pltpu.VMEM((2, 4, 4, ROWS, 256), BF16),
            pltpu.VMEM((2, 4, 4, ROWS, 128), BF16),
            pltpu.VMEM((2, 4, 4, ROWS, 128), BF16),
            pltpu.VMEM((4, ROWS, 128), F32),
            pltpu.VMEM((4, ROWS, 128), F32),
            pltpu.VMEM((4, ROWS, 128), F32),
            pltpu.VMEM((4, ROWS, 128), F32),
            pltpu.VMEM((ROWS, 512), BF16),
            pltpu.VMEM((ROWS, 2048), BF16),
            pltpu.VMEM((5, ROWS, ROWS), BF16),
            pltpu.VMEM((5, ROWS, ROWS), BF16),
            pltpu.VMEM((NB, 512, 512), F32),
            pltpu.VMEM((NB, 4, 4, 32, 512), BF16),
            pltpu.VMEM((NB, 4, 4, 32, 512), BF16),
            pltpu.VMEM((2, 3, NB, 4, 32, 256), BF16),
            pltpu.VMEM((NB, 4, 32, 256), BF16),
            pltpu.VMEM((NB, 4, 32, 256), BF16),
            pltpu.VMEM((3, NB, 32, 256), BF16),
            pltpu.VMEM((3, NB, 32, 256), BF16),
            pltpu.VMEM((4, NB, 8, 512), F32),
            pltpu.VMEM((3, NB, 8, 512), F32),
            dma((9,)), dma((10,)), dma((8,)), dma((8,)),
            dma((8,)), dma((10,)), dma((8,)), dma((8,)),
            dma((10,)), dma((8,)),
            dma((NB,)), dma((NB,)), dma((3, 6)), dma((3, 6)), dma((3, 6)), dma((3, 3)),
        ],
        compiler_params=pltpu.CompilerParams(
            collective_id=0, has_side_effects=True, vmem_limit_bytes=67043328),
    )(tokens_in[0], user_ids, w_in, w_out, cotangent[0])
    output, grad_tokens, total_in, total_out = finish(output, grad_tokens, total_in, total_out)
    return output, grad_tokens, total_in, total_out.T


def solution(mesh):
    in_specs = (P("dp", "seq", None), P("dp", None), P(), P(), P("dp", "seq", None))
    out_specs = (
        P("dp", "seq", None),
        P("dp", "seq", None),
        P(("dp", "seq"), None),
        P(None, ("dp", "seq")),
    )
    return jax.shard_map(local, mesh=mesh, in_specs=in_specs, out_specs=out_specs, check_vma=False)
```

```python
import math

import jax
import jax.numpy as jnp
from jax import lax
from jax.experimental import pallas as pl
from jax.experimental.pallas import tpu as pltpu
from jax.sharding import PartitionSpec as P

HEADS = 4
HD = 128
ROWS = 512
F32 = jnp.float32
BF16 = jnp.bfloat16
EPS = 1e-05
HALF_SCALE = 0.5 / math.sqrt(HD)
MESH = pl.DeviceIdType.MESH
NB = 5
GROUPS = ((0, 2), (2, 1), (3, 1), (4, 1))

OWN_MOVES = (
    (0, 1, 0, (0, 1, 2, 3)),
    (0, 3, 0, (0, 1)),
    (1, 2, 1, (1, 2, 3)),
    (1, 0, 1, (0, 1, 2)),
    (2, 3, 2, (0, 1, 2, 3)),
)
RELAYS = {
    (1, 0, 2): 2, (1, 0, 3): 2,
    (0, 1, 0): 3, (0, 1, 1): 3, (0, 1, 2): 3,
    (3, 0, 0): 2, (3, 0, 1): 2, (3, 1, 0): 2,
    (2, 1, 3): 3,
}
ARRIVALS = {
    0: ((1, 0), (1, 1), (1, 2)),
    1: ((0, 0), (0, 1), (0, 2), (0, 3)),
    2: ((1, 1), (0, 0), (1, 2), (0, 1), (1, 3), (1, 0), (0, 2), (0, 3)),
    3: ((2, 0), (0, 0), (2, 1), (0, 1), (2, 2), (1, 0), (2, 3), (1, 1), (1, 2), (1, 3)),
}
STEPS = 10
QUERY_MOVES = (
    (0, 1, 0, (0, 1)),
    (0, 3, 0, (2, 3)),
    (1, 2, 1, (0, 1, 2, 3)),
    (2, 3, 2, (0, 1, 2, 3)),
    (1, 0, 1, (3, 2)),
    (0, 1, 0, (2, 3)),
)
QUERY_RELAYS = {
    (1, 0, 0): 2, (1, 0, 1): 2,
    (3, 0, 2): 2, (3, 0, 3): 2,
    (2, 1, 0): 3, (2, 1, 1): 3,
    (0, 1, 3): 3, (0, 1, 2): 3,
}
QUERY_ARRIVALS = {
    0: ((1, 3), (1, 2)),
    1: ((0, 0), (0, 1), (0, 2), (0, 3)),
    2: ((1, 0), (1, 1), (1, 2), (1, 3), (0, 2), (0, 3), (0, 0), (0, 1)),
    3: ((0, 2), (0, 3), (2, 0), (2, 1), (2, 2), (2, 3), (1, 0), (1, 1), (1, 3), (1, 2)),
}
GRAD_ARRIVALS = {
    0: ((1, 0), (1, 1), (1, 2)),
    1: ((0, 0), (0, 1), (0, 2), (0, 3)),
    2: ((1, 1), (1, 2), (0, 0), (1, 3), (0, 2), (0, 1), (0, 3), (1, 0)),
    3: ((2, 0), (2, 1), (0, 0), (2, 2), (0, 1), (2, 3), (1, 0), (1, 1), (1, 3), (1, 2)),
}


def place():
    dp, seq = lax.axis_index("dp"), lax.axis_index("seq")
    return dp // 4, dp % 4, seq // 2, seq % 2


def device(y, x, z, core):
    return {"dp": y * 4 + x, "seq": z * 2 + core}


def turn(i, d):
    return lax.rem(i + d, 4)


def remote(src, dst, send, recv, target):
    return pltpu.make_async_remote_copy(
        src_ref=src, dst_ref=dst, send_sem=send, recv_sem=recv,
        device_id=target, device_id_type=MESH)


def dot_nn(a, b):
    return jnp.dot(a, b, preferred_element_type=F32)


def dot_nt(a, b):
    return lax.dot_general(a, b, (((1,), (1,)), ((), ())), preferred_element_type=F32)


def dot_tn(a, b):
    return lax.dot_general(a, b, (((0,), (0,)), ((), ())), preferred_element_type=F32)


class Gather:
    def __init__(self, buf, sems, chip, core, target, moves, relays, arrivals):
        self.buf, self.near, self.far = buf, buf.at[0], buf.at[1]
        self.ss, self.rs, self.sp, self.rp = sems
        self.chip, self.core, self.target = chip, core, target
        self.moves, self.relays, self.arrivals = moves, relays, arrivals
        self.sent = {}
        for role in range(4):
            mine = [(receiver, owner, h) for sender, receiver, owner, heads in moves if sender == role for h in heads]
            mine += [(receiver, owner, h) for (sender, owner, h), receiver in relays.items() if sender == role]
            for k, (receiver, owner, h) in enumerate(mine):
                self.sent[role, receiver, owner, h] = k

    def move(self, sender, receiver, owner, h):
        return remote(self.near.at[owner, h], self.near.at[owner, h], self.ss.at[self.sent[sender, receiver, owner, h]],
                      self.rs.at[self.arrivals[receiver].index((owner, h))], self.target(receiver, self.core))

    def landed(self, step, owner, h):
        here = self.near.at[owner, h]
        return remote(here, here, self.ss.at[0], self.rs.at[step], self.target(turn(self.chip, 1), self.core))

    def share(self, owner, h):
        k = jnp.where(self.chip - owner == 1, 4, 0) + h
        return remote(self.near.at[owner, h], self.far.at[owner, h], self.sp.at[k],
                      self.rp.at[k], self.target(self.chip, 1 - self.core))

    def start(self, moves=None, share=True, only=(0, 1, 2, 3)):
        if share:
            @pl.when(self.core == 0)
            def _():
                for h in only:
                    self.share(self.chip, h).start()
        for sender, receiver, owner, heads in (self.moves if moves is None else moves):
            @pl.when(self.chip == sender)
            def _():
                for h in heads:
                    if h in only:
                        self.move(sender, receiver, owner, h).start()

    def arrive(self, step, roles=(0, 1, 2, 3)):
        for role in roles:
            order = self.arrivals.get(role, ())
            if step >= len(order):
                continue
            owner, h = order[step]

            @pl.when(self.chip == role)
            def _():
                self.landed(step, owner, h).wait_recv()
                if (role, owner, h) in self.relays:
                    self.move(role, self.relays[role, owner, h], owner, h).start()
                if owner == role - 1:
                    self.share(owner, h).start()
                if owner == role - 2:
                    @pl.when(self.core == 1)
                    def _():
                        self.share(owner, h).start()

    def look(self, step):
        code = jnp.int32(-1)
        for role, order in self.arrivals.items():
            for k, (owner, h) in enumerate(order):
                dest = self.relays.get((role, owner, h), -1)
                value = owner * 4 + h
                if dest >= 0:
                    there = self.arrivals[dest].index((owner, h))
                    value += 16 * (dest + 1) + 128 * there + 2048 * self.sent[role, dest, owner, h]
                code = jnp.where((self.chip == role) & (step == k), value, code)
        return (code >= 0, (code // 4) % 4, code % 4, (code // 16) % 8 - 1, (code // 128) % 16, code // 2048)

    def service(self, step, serve=None):
        wanted, owner, h, dest, there, k = self.look(step)
        if serve is not None:
            wanted = wanted & serve

        @pl.when(wanted)
        def _():
            here = self.near.at[owner, h]
            gap = self.chip - owner
            self.landed(step, owner, h).wait_recv()

            @pl.when(dest >= 0)
            def _():
                remote(here, here, self.ss.at[k], self.rs.at[there], self.target(dest, self.core)).start()

            @pl.when((gap == 1) | ((gap == 2) & (self.core == 1)))
            def _():
                self.share(owner, h).start()

    def drain(self):
        @pl.when(self.core == 0)
        def _():
            for h in range(HEADS):
                self.share(self.chip, h).wait_send()
        for sender, receiver, owner, heads in self.moves:
            @pl.when(self.chip == sender)
            def _():
                for h in heads:
                    self.move(sender, receiver, owner, h).wait_send()
        for (role, owner, h), receiver in self.relays.items():
            @pl.when(self.chip == role)
            def _():
                self.move(role, receiver, owner, h).wait_send()
        for role, order in self.arrivals.items():
            for owner, h in order:
                if owner == role - 1:
                    @pl.when(self.chip == role)
                    def _():
                        self.share(owner, h).wait_send()
                if owner == role - 2:
                    @pl.when((self.chip == role) & (self.core == 1))
                    def _():
                        self.share(owner, h).wait_send()


def layer_kernel(tokens_hbm, ids, w_in_hbm, w_out_hbm, cot_hbm, output_hbm, grad_tokens_hbm, out_in_hbm, out_out_hbm,
                 out_in, out_out, output, grad_tokens, out_sems, tokens, w_in, w_out, cot, in_sems, normed_t, cot_t, normed, slope, u, kv, qs, gs, att, dq, dk, dv, gated, gh, masks, masks_t,
                 part, s2, recv1, r2, s3a, s3b, r3a, r3b, t4, r4,
                 kss, krs, ksp, krp, qss, qrs, qsp, qrp, grs, grp,
                 ss1, rs1, sss, rs2, rs3, rs4):
    y, x, z, c = place()
    other = 1 - c
    block = z * 2 + c
    peers = ([device(y, x, z, other)]
             + [device(y, turn(x, d), z, c) for d in (1, 2, 3)]
             + [device(turn(y, d), x, z, c) for d in (1, 2, 3)]
             + [device(y, x, turn(z, d), c) for d in (1, 2, 3)])
    barrier = pltpu.get_barrier_semaphore()
    for t in peers:
        pl.semaphore_signal(barrier, inc=1, device_id=t, device_id_type=MESH)

    tokens_in = pltpu.make_async_copy(tokens_hbm, tokens, in_sems.at[0])
    tokens_in.start()
    w_ins = {}
    for i, col in enumerate((1536, 512, 1024, 0)):
        cols = pl.ds(col, 512)
        w_ins[col] = pltpu.make_async_copy(w_in_hbm.at[:, cols], w_in.at[:, cols], in_sems.at[1 + i])
        w_ins[col].start()
    cot_in = pltpu.make_async_copy(cot_hbm, cot, in_sems.at[5])
    w_out_in = pltpu.make_async_copy(w_out_hbm, w_out, in_sems.at[6])
    cot_in.start()
    w_out_in.start()
    mz, mc = 3 - z, 1 - c

    def mirrored(zz, cc):
        return device(y, x, 3 - zz, 1 - cc)

    before = Gather(kv, (kss, krs, ksp, krp), z, c, lambda zz, cc: device(y, x, zz, cc),
                    OWN_MOVES, RELAYS, ARRIVALS)
    queries = Gather(qs, (qss, qrs, qsp, qrp), mz, mc, mirrored,
                     QUERY_MOVES, QUERY_RELAYS, QUERY_ARRIVALS)
    grads = Gather(gs, (kss, grs, ksp, grp), mz, mc, mirrored,
                   OWN_MOVES, RELAYS, GRAD_ARRIVALS)

    def stats(v):
        center = v - jnp.mean(v, axis=-1, keepdims=True)
        inverse = lax.rsqrt(jnp.mean(center * center, axis=-1, keepdims=True) + EPS)
        return center * inverse, inverse

    def row_loop(size):
        def wrap(body):
            @pl.loop(0, ROWS // size)
            def _(i):
                body(pl.ds(pl.multiple_of(i * size, size), size))
        return wrap

    tokens_in.wait()

    @row_loop(128)
    def _(rows):
        normed[rows, :] = stats(tokens[rows, :].astype(F32))[0].astype(BF16)

    def features(col, width, put):
        @row_loop(256)
        def _(rows):
            half = 0.5 * dot_nn(normed[rows, :], w_in[:, col:col + width])
            t = jnp.tanh(half)
            slope[rows, col:col + width] = 0.5 * (1.0 + t) * (1.0 + half * (1.0 - t))
            put(rows, (half * (1.0 + t)).astype(BF16))

    def put_kv(first, at):
        def put(rows, a):
            for h in range(2):
                kv[0, z, first + h, rows, at:at + 128] = a[:, h * 128:(h + 1) * 128]
        return put

    def put_q(rows, a):
        for h in range(HEADS):
            qs[0, mz, h, rows, :] = a[:, h * 128:(h + 1) * 128]

    def put_u(rows, a):
        u[rows, :] = a

    w_ins[1536].wait()
    features(1536, 256, put_kv(0, 0))
    w_ins[512].wait()
    features(512, 256, put_kv(0, 128))
    pl.semaphore_wait(barrier, len(peers))
    before.start(only=(0, 1))
    features(1792, 256, put_kv(2, 0))
    features(768, 256, put_kv(2, 128))
    before.start(only=(2, 3))
    w_ins[1024].wait()
    features(1024, 512, put_q)
    queries.start(QUERY_MOVES[:4])
    w_ins[0].wait()
    features(0, 512, put_u)

    def ids_of(b):
        b = jnp.clip(b, 0, 7)
        return ids[:, pl.ds(pl.multiple_of(b * ROWS, ROWS), ROWS)].astype(F32)

    own_ids = jnp.transpose(jnp.broadcast_to(ids_of(block), (128, ROWS)))
    own_col = jnp.broadcast_to(own_ids[:, 0:1], (ROWS, ROWS))
    one, nil = jnp.ones((ROWS, ROWS), F32), jnp.zeros((ROWS, ROWS), F32)
    down = lax.broadcasted_iota(jnp.int32, (ROWS, ROWS), 0)
    right = lax.broadcasted_iota(jnp.int32, (ROWS, ROWS), 1)
    for d in range(5):
        same = own_col == jnp.broadcast_to(ids_of(block - d), (ROWS, ROWS))
        same_t = own_col == jnp.broadcast_to(ids_of(block + d), (ROWS, ROWS))
        if d == 0:
            same = same & (right <= down)
            same_t = same_t & (down <= right)
        masks[d] = jnp.where(same, one, nil).astype(BF16)
        masks_t[d] = jnp.where(same_t, one, nil).astype(BF16)

    def pipeline(items, scores, weigh, add):
        ahead = scores(*items[0])
        for i, item in enumerate(items):
            now = ahead
            if i + 1 < len(items):
                ahead = scores(*items[i + 1])
            add(item, weigh(now, item))

    def tiles(where, flip, heads, d):
        out = []
        for h in heads:
            for r in (0, 256):
                cols = (0, 512)
                if isinstance(d, int) and d == 0:
                    cols = ((0, 256), (0, 512))[r // 256] if not flip else ((0, 512), (256, 512))[r // 256]
                out.append(where + (h, d, (r, r + 256), cols))
        return out

    def forward_tiles(items, first=False):
        def scores(e, o, h, d, rows, cols):
            return dot_nt(qs[0, mz, h, rows[0]:rows[1], :], kv[e, o, h, cols[0]:cols[1], 0:128])

        def weigh(now, item):
            e, o, h, d, rows, cols = item
            half = (now * HALF_SCALE).astype(BF16)
            return (half + half * jnp.tanh(half)) * masks[d, rows[0]:rows[1], cols[0]:cols[1]]

        def add(item, w):
            e, o, h, d, rows, cols = item
            a = dot_nn(w, kv[e, o, h, cols[0]:cols[1], 128:256])
            if first:
                att[h, rows[0]:rows[1], :] = a
            else:
                att[h, rows[0]:rows[1], :] += a

        pipeline(items, scores, weigh, add)

    def query_tiles(items, first=False):
        def scores(e, o, h, d, rows, cols):
            keys = slice(cols[0], cols[1])
            mine = slice(rows[0], rows[1])
            return (dot_nt(qs[0, mz, h, mine, :], kv[e, o, h, keys, 0:128]),
                    dot_nt(gs[0, mz, h, mine, :], kv[e, o, h, keys, 128:256]))

        def weigh(now, item):
            e, o, h, d, rows, cols = item
            half = (now[0] * HALF_SCALE).astype(BF16)
            t = jnp.tanh(half)
            a = (t + 1) * masks[d, rows[0]:rows[1], cols[0]:cols[1]]
            return now[1].astype(BF16) * (a + half * a * (1 - t))

        def add(item, ds):
            e, o, h, d, rows, cols = item
            a = dot_nn(ds, kv[e, o, h, cols[0]:cols[1], 0:128])
            if first:
                dq[h, rows[0]:rows[1], :] = a
            else:
                dq[h, rows[0]:rows[1], :] += a

        pipeline(items, scores, weigh, add)

    def key_tiles(items, first=False):
        def scores(e, o, h, d, rows, cols):
            theirs = slice(cols[0], cols[1])
            mine = slice(rows[0], rows[1])
            return (dot_nt(kv[0, z, h, mine, 0:128], qs[e, o, h, theirs, :]),
                    dot_nt(kv[0, z, h, mine, 128:256], gs[e, o, h, theirs, :]))

        def weigh(now, item):
            e, o, h, d, rows, cols = item
            half = (now[0] * HALF_SCALE).astype(BF16)
            t = jnp.tanh(half)
            a = (t + 1) * masks_t[d, rows[0]:rows[1], cols[0]:cols[1]]
            w = half * a
            return w, now[1].astype(BF16) * (a + w * (1 - t))

        def add(item, got):
            e, o, h, d, rows, cols = item
            av = dot_nn(got[0], gs[e, o, h, cols[0]:cols[1], :])
            ak = dot_nn(got[1], qs[e, o, h, cols[0]:cols[1], :])
            if first:
                dv[h, rows[0]:rows[1], :] = av
                dk[h, rows[0]:rows[1], :] = ak
            else:
                dv[h, rows[0]:rows[1], :] += av
                dk[h, rows[0]:rows[1], :] += ak

        pipeline(items, scores, weigh, add)

    def meet(gather, step, compute, flip, also=None):
        there, o, h, _, _, _ = gather.look(step)
        gap = gather.chip - o
        even = 2 * gap
        odd = even + 2 * gather.core - 1

        @pl.when(there & ((gap == 1) | ((gap == 2) & (gather.core == 0))))
        def _():
            gather.share(o, h).wait_recv()
            if also is not None:
                also.share(o, h).wait_recv()
            compute(tiles((0, o), flip, (h,), even) + tiles((1, o), flip, (h,), odd))

        @pl.when(there & (gap == 2) & (gather.core == 1))
        def _():
            compute(tiles((0, o), flip, (h,), even))

    def beside(gather, compute, flip, also=None):
        @pl.when(gather.core == 1)
        def _():
            @pl.loop(0, 2)
            def _(pair):
                heads = (2 * pair, 2 * pair + 1)
                for h in heads:
                    gather.share(gather.chip, h).wait_recv()
                    if also is not None:
                        also.share(gather.chip, h).wait_recv()
                compute(tiles((1, gather.chip), flip, heads, 1))

    def pair_copy(b):
        return remote(s2.at[b], recv1.at[b], ss1.at[b], rs1.at[b], device(y, x, z, other))

    def weight(b, left, cols):
        ahead = dot_nn(left[0:256, :], cols)
        for r in range(4):
            now = ahead.reshape(16, 2, 8, 512)
            if r < 3:
                ahead = dot_nn(left[(r + 1) * 256:(r + 2) * 256, :], cols)
            even, odd = now[:, 0].reshape(128, 512), now[:, 1].reshape(128, 512)
            part[b, r * 128:(r + 1) * 128, :] = jnp.where(c == 0, even, odd)
            s2[b, r] = jnp.where(c == 0, odd, even).reshape(4, 32, 512).astype(BF16)
        pair_copy(b).start()

    def plane_copies(g):
        b = pl.ds(*GROUPS[g])
        out = []
        for d in (1, 2, 3):
            xx, yy = turn(x, d), turn(y, d)
            out.append(remote(s2.at[b, :, xx, :, pl.ds(0, 256)], r2.at[0, d - 1, b], sss.at[g, d - 1],
                              rs2.at[g, d - 1], device(y, xx, z, c)))
            out.append(remote(s2.at[b, yy, :, :, pl.ds(256, 256)], r2.at[1, d - 1, b], sss.at[g, d + 2],
                              rs2.at[g, d + 2], device(yy, x, z, c)))
        return out

    def line_copies(g):
        b = pl.ds(*GROUPS[g])
        out = []
        for d in (1, 2, 3):
            xx, yy = turn(x, d), turn(y, d)
            out.append(remote(s3a.at[b, yy], r3a.at[d - 1, b], sss.at[g, d - 1], rs3.at[g, d - 1],
                              device(yy, x, z, c)))
            out.append(remote(s3b.at[b, xx], r3b.at[d - 1, b], sss.at[g, d + 2], rs3.at[g, d + 2],
                              device(y, xx, z, c)))
        return out

    def chip_copies(g):
        b = pl.ds(*GROUPS[g])
        return [remote(t4.at[turn(z, d), b], r4.at[d - 1, b], sss.at[g, d - 1], rs4.at[g, d - 1],
                       device(y, x, turn(z, d), c)) for d in (1, 2, 3)]

    def blocks_of(g):
        return range(GROUPS[g][0], GROUPS[g][0] + GROUPS[g][1])

    def second(g):
        for b in blocks_of(g):
            pair_copy(b).wait()
            for i in range(4):
                mine = part[b, i * 128:(i + 1) * 128, :].reshape(4, 32, 512)
                s2[b, i] = (mine + recv1[b, i].astype(F32)).astype(BF16)
        for cp in plane_copies(g):
            cp.start()

    def third(g):
        for cp in plane_copies(g):
            cp.wait()
        for b in blocks_of(g):
            a = s2[b, :, x, :, 0:256].astype(F32)
            e = s2[b, y, :, :, 256:512].astype(F32)
            for d in range(3):
                a = a + r2[0, d, b].astype(F32)
                e = e + r2[1, d, b].astype(F32)
            s3a[b] = a.astype(BF16)
            s3b[b] = e.astype(BF16)
        for cp in line_copies(g):
            cp.start()

    def fourth(g):
        for cp in line_copies(g):
            cp.wait()
        for b in blocks_of(g):
            a = s3a[b, y].astype(F32)
            e = s3b[b, x].astype(F32)
            for d in range(3):
                a = a + r3a[d, b].astype(F32)
                e = e + r3b[d, b].astype(F32)
            t4[:, b, :, 0:256] = a.reshape(4, 8, 256)
            t4[:, b, :, 256:512] = e.reshape(4, 8, 256)
        for cp in chip_copies(g):
            cp.start()

    RESULT = {1: 0, 2: 1024, 3: 512, 4: 1536}

    def result_copy(b):
        if b == 0:
            return pltpu.make_async_copy(out_out, out_out_hbm, out_sems.at[2])
        cols = pl.ds(RESULT[b], 512)
        return pltpu.make_async_copy(out_in.at[:, cols], out_in_hbm.at[:, cols], out_sems.at[2 + b])

    def fifth(g):
        for cp in chip_copies(g):
            cp.wait()
        for b in blocks_of(g):
            total = t4[z, b] + r4[0, b] + r4[1, b] + r4[2, b]
            if b == 0:
                out_out[...] = total
            else:
                out_in[:, RESULT[b]:RESULT[b] + 512] = total
            result_copy(b).start()

    forward_tiles(tiles((0, z), False, range(HEADS), 0), first=True)
    cot_in.wait()
    w_out_in.wait()

    @row_loop(128)
    def _(rows):
        normed_t[:, rows] = jnp.transpose(normed[rows, :])
        cot_t[:, rows] = jnp.transpose(cot[rows, :])

    beside(before, forward_tiles, False)
    before.service(0)
    before.service(1)
    for step in range(2):
        queries.arrive(step, roles=(1, 2, 3))

    @pl.loop(0, STEPS)
    def _(step):
        meet(before, step, forward_tiles, False)
        before.service(step + 2)

        @pl.when(step == 3)
        def _():
            queries.start(QUERY_MOVES[4:], share=False)


    @row_loop(256)
    def _(rows):
        a = jnp.concatenate([att[h, rows, :] for h in range(HEADS)], axis=1)
        no, inverse = stats(a)
        uu = u[rows, :].astype(F32)
        g = (no * uu).astype(BF16)
        gated[rows, :] = g
        gg = dot_nt(cot[rows, :], w_out[...])
        gh[rows, 0:512] = (gg * no * slope[rows, 0:512]).astype(BF16)
        gn = gg * uu
        back = inverse * (gn - jnp.mean(gn, axis=-1, keepdims=True)
                          - no * jnp.mean(gn * no, axis=-1, keepdims=True))
        back = back.astype(BF16)
        for h in range(HEADS):
            gs[0, mz, h, rows, :] = back[:, h * 128:(h + 1) * 128]

    pl.when(mz < 3)(before.drain)
    grads.start()
    queries.arrive(0, roles=(0,))
    queries.arrive(1, roles=(0,))
    query_tiles(tiles((0, z), False, range(HEADS), 0), first=True)
    weight(0, cot_t, gated[...])
    weight(1, normed_t, gh[:, 0:512])
    queries.arrive(2, roles=(1,))
    early = mz < 2

    @pl.loop(1, 5)
    def _(d):
        @pl.when(block >= d)
        def _():
            owner = jnp.where(d % 2 == 0, z - d // 2, z - (d + 1) // 2 + c)
            query_tiles(tiles((d % 2, owner), False, range(HEADS), d))

        grads.service(d - 1, serve=early)

        @pl.when(d == 2)
        def _():
            second(0)

    queries.arrive(3, roles=(1,))

    @row_loop(256)
    def _(rows):
        for h in range(HEADS):
            at = 1024 + h * 128
            gh[rows, at:at + 128] = (dq[h, rows, :] * HALF_SCALE * slope[rows, at:at + 128]).astype(BF16)

    weight(2, normed_t, gh[:, 1024:1536])
    key_tiles(tiles((0, mz), True, range(HEADS), 0), first=True)
    beside(grads, key_tiles, True, also=queries)
    second(1)
    late = mz >= 2
    pl.when(mz == 3)(before.drain)
    grads.service(0, serve=late)
    for step in range(2, 8):
        queries.arrive(step, roles=(2,))
    for step in range(2, 8):
        queries.arrive(step, roles=(3,))

    @pl.loop(0, STEPS)
    def _(step):
        grads.service(step + 1, serve=late)

        @pl.when(step == 3)
        def _():
            third(0)

        @pl.when(step == 4)
        def _():
            queries.arrive(8, roles=(3,))
            queries.arrive(9, roles=(3,))

        meet(grads, step, key_tiles, True, also=queries)

    @row_loop(256)
    def _(rows):
        for h in range(HEADS):
            at = 512 + h * 128
            gh[rows, at:at + 128] = (dv[h, rows, :] * slope[rows, at:at + 128]).astype(BF16)
            at = 1536 + h * 128
            gh[rows, at:at + 128] = (dk[h, rows, :] * HALF_SCALE * slope[rows, at:at + 128]).astype(BF16)

    weight(3, normed_t, gh[:, 512:1024])
    weight(4, normed_t, gh[:, 1536:2048])
    third(1)
    second(2)
    second(3)

    @row_loop(256)
    def _(rows):
        up = dot_nt(gh[rows, :], w_in[...])
        zhat, inverse = stats(tokens[rows, :].astype(F32))
        back = inverse * (up - jnp.mean(up, axis=-1, keepdims=True)
                          - zhat * jnp.mean(up * zhat, axis=-1, keepdims=True))
        grad_tokens[rows, :] = (back + cot[rows, :].astype(F32)).astype(BF16)

    tokens_out = pltpu.make_async_copy(grad_tokens, grad_tokens_hbm, out_sems.at[1])
    tokens_out.start()
    fourth(0)
    fourth(1)

    @row_loop(256)
    def _(rows):
        output[rows, :] = (dot_nn(gated[rows, :], w_out[...]) + tokens[rows, :].astype(F32)).astype(BF16)

    output_out = pltpu.make_async_copy(output, output_hbm, out_sems.at[0])
    output_out.start()
    third(2)
    third(3)
    fifth(0)
    fifth(1)
    fourth(2)
    fourth(3)
    queries.drain()
    grads.drain()
    output_out.wait()
    tokens_out.wait()
    fifth(2)
    fifth(3)
    for b in range(NB):
        result_copy(b).wait()


def finish_kernel(a, b, p, q, out_a, out_b, out_p, out_q, va, vb, vp, vq, ins, outs):
    moves = []
    for i in range(4):
        rows = pl.ds(i * 128, 128)
        moves.append((a.at[rows, :], va.at[rows, :], out_a.at[0, rows, :]))
        moves.append((b.at[rows, :], vb.at[rows, :], out_b.at[0, rows, :]))
    moves.append((p, vp, out_p))
    fetch = [pltpu.make_async_copy(q, vq, ins.at[9])]
    fetch += [pltpu.make_async_copy(src, mid, ins.at[i]) for i, (src, mid, _) in enumerate(moves)]
    store = [pltpu.make_async_copy(mid, dst, outs.at[i]) for i, (_, mid, dst) in enumerate(moves)]
    last = pltpu.make_async_copy(vq, out_q, outs.at[9])
    for cp in fetch:
        cp.start()
    fetch[0].wait()
    last.start()
    for got, put in zip(fetch[1:], store):
        got.wait()
        put.start()
    for put in store:
        put.wait()
    last.wait()


def finish(output, grad_tokens, total_in, total_out):
    hbm = pl.BlockSpec(memory_space=pl.ANY)
    dma = pltpu.SemaphoreType.DMA
    return pl.pallas_call(
        finish_kernel,
        name="finish",
        out_shape=(
            jax.ShapeDtypeStruct((1, ROWS, 1024), BF16),
            jax.ShapeDtypeStruct((1, ROWS, 1024), BF16),
            jax.ShapeDtypeStruct((8, 2048), F32),
            jax.ShapeDtypeStruct((8, 512), F32),
        ),
        in_specs=[hbm] * 4,
        out_specs=(hbm,) * 4,
        scratch_shapes=[
            pltpu.VMEM((ROWS, 1024), BF16),
            pltpu.VMEM((ROWS, 1024), BF16),
            pltpu.VMEM((8, 2048), F32),
            pltpu.VMEM((8, 512), F32),
            dma((10,)), dma((10,)),
        ],
    )(output, grad_tokens, total_in, total_out)


def local(tokens_in, user_ids, w_in, w_out, cotangent):
    vmem = pl.BlockSpec(memory_space=pltpu.VMEM)
    hbm = pl.BlockSpec(memory_space=pl.ANY)
    dma = pltpu.SemaphoreType.DMA

    output, grad_tokens, total_in, total_out = pl.pallas_call(
        layer_kernel,
        name="layer",
        out_shape=(
            jax.ShapeDtypeStruct((ROWS, 1024), BF16),
            jax.ShapeDtypeStruct((ROWS, 1024), BF16),
            jax.ShapeDtypeStruct((8, 2048), F32),
            jax.ShapeDtypeStruct((8, 512), F32),
        ),
        in_specs=[hbm, vmem, hbm, hbm, hbm],
        out_specs=(hbm,) * 4,
        scratch_shapes=[
            pltpu.VMEM((8, 2048), F32),
            pltpu.VMEM((8, 512), F32),
            pltpu.VMEM((ROWS, 1024), BF16),
            pltpu.VMEM((ROWS, 1024), BF16),
            dma((7,)),
            pltpu.VMEM((ROWS, 1024), BF16),
            pltpu.VMEM((1024, 2048), BF16),
            pltpu.VMEM((512, 1024), BF16),
            pltpu.VMEM((ROWS, 1024), BF16),
            dma((7,)),
            pltpu.VMEM((1024, ROWS), BF16),
            pltpu.VMEM((1024, ROWS), BF16),
            pltpu.VMEM((ROWS, 1024), BF16),
            pltpu.VMEM((ROWS, 2048), F32),
            pltpu.VMEM((ROWS, 512), BF16),
            pltpu.VMEM((2, 4, 4, ROWS, 256), BF16),
            pltpu.VMEM((2, 4, 4, ROWS, 128), BF16),
            pltpu.VMEM((2, 4, 4, ROWS, 128), BF16),
            pltpu.VMEM((4, ROWS, 128), F32),
            pltpu.VMEM((4, ROWS, 128), F32),
            pltpu.VMEM((4, ROWS, 128), F32),
            pltpu.VMEM((4, ROWS, 128), F32),
            pltpu.VMEM((ROWS, 512), BF16),
            pltpu.VMEM((ROWS, 2048), BF16),
            pltpu.VMEM((5, ROWS, ROWS), BF16),
            pltpu.VMEM((5, ROWS, ROWS), BF16),
            pltpu.VMEM((NB, 512, 512), F32),
            pltpu.VMEM((NB, 4, 4, 32, 512), BF16),
            pltpu.VMEM((NB, 4, 4, 32, 512), BF16),
            pltpu.VMEM((2, 3, NB, 4, 32, 256), BF16),
            pltpu.VMEM((NB, 4, 32, 256), BF16),
            pltpu.VMEM((NB, 4, 32, 256), BF16),
            pltpu.VMEM((3, NB, 32, 256), BF16),
            pltpu.VMEM((3, NB, 32, 256), BF16),
            pltpu.VMEM((4, NB, 8, 512), F32),
            pltpu.VMEM((3, NB, 8, 512), F32),
            dma((9,)), dma((10,)), dma((8,)), dma((8,)),
            dma((8,)), dma((10,)), dma((8,)), dma((8,)),
            dma((10,)), dma((8,)),
            dma((NB,)), dma((NB,)), dma((4, 6)), dma((4, 6)), dma((4, 6)), dma((4, 3)),
        ],
        compiler_params=pltpu.CompilerParams(
            collective_id=0, has_side_effects=True, vmem_limit_bytes=67043328),
    )(tokens_in[0], user_ids, w_in, w_out, cotangent[0])
    output, grad_tokens, total_in, total_out = finish(output, grad_tokens, total_in, total_out)
    return output, grad_tokens, total_in, total_out.T


def solution(mesh):
    in_specs = (P("dp", "seq", None), P("dp", None), P(), P(), P("dp", "seq", None))
    out_specs = (
        P("dp", "seq", None),
        P("dp", "seq", None),
        P(("dp", "seq"), None),
        P(None, ("dp", "seq")),
    )
    return jax.shard_map(local, mesh=mesh, in_specs=in_specs, out_specs=out_specs, check_vma=False)
```
